32 devices in a mesh: spin: 2 (over core), band: 16 (over z, y, x).
Axes of the slice: x: 2, y: 2, z: 4, core: 2. Of those that a mesh axis runs over, the one named last changes fastest.
Arguments:
- orbitals: bfloat16 [128, 512000], P(('spin', 'band')), parts along dimension 0, may hold values from -40 to 40
Outputs:
- projector: float32 [32, 512000], P('spin', 'band'), parts along dimension 0
The draws below stay inside these ranges and needn't reach their ends.
There are 2 independent parts, one for each index of `spin`. The reference program is written for one: setup_inputs(seed, part) draws one part's arguments, and reference() takes and returns one part's arrays. A program takes and returns all parts, laid end to end along the dimension named above; each array names one. Nothing has to cross between parts.
All inputs are finite; a program needn't handle non-finite values.
Results may differ from the reference program's by a relative error of at most 0.0003.
Values may be sent and summed in bfloat16 or wider, within the bound.
A program may use at most 512 MiB of HBM per device.

```python
import math
import jax
import jax.numpy as jnp
from jax import lax

NG = 80
OWN = 4
NP = 2
NB = 64
N_BAND = 16


def draw_orbitals(key, part):
    total = NG ** 3
    common_key = jax.random.fold_in(key, 11)
    single_key = jax.random.fold_in(key, 12)
    scale_key = jax.random.fold_in(key, 13)
    planes = (jnp.arange(total, dtype=jnp.int32) // (NG * NG)).astype(jnp.float32) / NG
    common = jax.random.truncated_normal(common_key, -4.0, 4.0, (total,), jnp.float32)
    single = jax.random.truncated_normal(single_key, -4.0, 4.0, (NB, total), jnp.float32)
    amplitude = jnp.exp(jax.random.uniform(scale_key, (NB,), jnp.float32, math.log(0.5), math.log(2.0)))
    envelope = jnp.exp(0.55 * planes)
    values = amplitude[:, None] * envelope[None, :] * (0.7 * common[None, :] + single)
    return values.astype(jnp.bfloat16)


def setup_inputs(seed: int = 0, part: int = 0) -> dict:
    splits = jax.random.split(jax.random.key(seed), 2)
    part_keys = jax.random.split(jax.random.fold_in(splits[1], part), 2)
    return {
        "orbitals": draw_orbitals(jax.random.fold_in(jax.random.fold_in(splits[1], part), 71), part),
    }


def reference(orbitals):
    total = NG ** 3
    stride = N_BAND // NP
    grouped = orbitals.reshape(N_BAND, OWN, total)
    targets = grouped[:, 0].astype(jnp.float32)
    partners = grouped[::stride, OWN - 1].astype(jnp.float32)
    indices = jnp.arange(NG, dtype=jnp.int32)
    folded = jnp.minimum(indices, NG - indices).astype(jnp.float32)
    wavenumber = 2.0 * jnp.pi / NG * folded
    squares = wavenumber * wavenumber
    nyquist = NG // 2 + 1
    totals = squares[:, None, None] + squares[None, :, None] + squares[None, None, :nyquist]
    kernel = jnp.where(totals > 0.0, 1.0 / (0.0025 + totals), 0.0)

    def one_target(target):
        densities = (target[None, :] * partners).reshape(NP, NG, NG, NG)
        spectrum = jnp.fft.rfftn(densities, axes=(1, 2, 3))
        potential = jnp.fft.irfftn(spectrum * kernel, s=(NG, NG, NG), axes=(1, 2, 3))
        return -jnp.sum(partners * potential.reshape(NP, total), axis=0)
    vectors = lax.map(one_target, targets)
    intersection = jnp.dot(targets, vectors.T, precision=lax.Precision.HIGHEST) / total
    metric = -0.5 * (intersection + intersection.T)
    factor = jnp.linalg.cholesky(metric)
    return jax.scipy.linalg.solve_triangular(factor, vectors, lower=True)
```

```python
import functools

import jax
import jax.numpy as jnp
import numpy as np
from jax import lax
from jax.experimental import pallas as pl
from jax.experimental.pallas import tpu as pltpu
from jax.sharding import PartitionSpec as P

NG = 80
NP = 2
PAD = 128
QUARTERS = 4
CHUNKS = 5
highest = lax.Precision.HIGHEST


def tables(length):
    indices = np.arange(length)
    nyquist = length // 2
    frequency = np.where(indices <= nyquist, indices, indices - nyquist)
    angles = 2.0 * np.pi / length * (frequency[:, None] * indices[None, :] % length)
    edges = (indices == 0) | (indices == nyquist)
    weights = np.where(edges, 1.0 / length, 2.0 / length)
    fourier = np.where((indices <= nyquist)[:, None], np.cos(angles), np.sin(angles))
    fourier = (fourier * np.sqrt(weights)[:, None]).astype(np.float32)
    squares = ((2.0 * np.pi / length * frequency) ** 2).astype(np.float32)
    return fourier, squares


def halves(table):
    high = table.astype(jnp.bfloat16)
    low = (table - high.astype(np.float32)).astype(jnp.bfloat16)
    return high, low


def left_table(table):
    high, low = halves(table)
    return np.concatenate([high, high, low], axis=1)


def right_table(table, depth):
    high, low = halves(table)
    result = np.zeros((depth, 2 * PAD), dtype=high.dtype)
    result[: table.shape[0], : table.shape[1]] = high
    result[: table.shape[0], PAD : PAD + table.shape[1]] = low
    return result


def barrier_all(me, count):
    barrier = pltpu.get_barrier_semaphore()
    for step in range(1, count):
        pl.semaphore_signal(
            barrier, inc=1, device_id={"band": lax.rem(me + step, count)},
            device_id_type=pl.DeviceIdType.MESH,
        )
    pl.semaphore_wait(barrier, count - 1)


def remote(source, target, send, receive, device):
    return pltpu.make_async_remote_copy(
        src_ref=source, dst_ref=target, send_sem=send, recv_sem=receive,
        device_id={"band": device}, device_id_type=pl.DeviceIdType.MESH,
    )


def share_kernel(count, row, partners, first_send, column_send, plane_send, receive, own_sem):
    me = lax.axis_index("band")
    planes = count // QUARTERS
    stride = count // NP
    column = lax.rem(me, QUARTERS)
    plane = lax.div(me, QUARTERS)
    base = plane * QUARTERS
    barrier_all(me, count)

    def first(r, q, c):
        return remote(row.at[q, c], partners.at[r, q, c], first_send.at[q - 1, c],
                      receive.at[r, q, c], lax.rem(me + q, count))

    def down(r, step, c):
        other = lax.rem(me + step * QUARTERS, count)
        return remote(partners.at[r, column, c], partners.at[r, column, c],
                      column_send.at[r, step - 1, c], receive.at[r, column, c], other)

    def neighbour(step):
        return base + lax.rem(column + step, QUARTERS)

    def across(r, step, c):
        return remote(partners.at[r, column, c], partners.at[r, column, c],
                      plane_send.at[r, step - 1, c], receive.at[r, column, c], neighbour(step))

    def arrived(r, q, c):
        remote(partners.at[r, q, c], partners.at[r, q, c], plane_send.at[r, 0, c],
               receive.at[r, q, c], me).wait_recv()

    for r in range(NP):
        @pl.when(me == r * stride)
        def _():
            own = pltpu.make_async_copy(row, partners.at[r], own_sem)
            own.start()
            own.wait()

    for c in range(CHUNKS):
        for r in range(NP):
            @pl.when(me != r * stride)
            def _():
                arrived(r, column, c)

            @pl.when(me == r * stride)
            def _():
                for q in range(1, QUARTERS):
                    first(r, q, c).start()

            @pl.when(plane == r * stride // QUARTERS)
            def _():
                for step in range(1, planes):
                    down(r, step, c).start()

            for step in range(1, QUARTERS):
                @pl.when(neighbour(step) != r * stride)
                def _():
                    across(r, step, c).start()

    for r in range(NP):
        @pl.when(me != r * stride)
        def _():
            for c in range(CHUNKS):
                for step in range(1, QUARTERS):
                    arrived(r, lax.rem(column + step, QUARTERS), c)

        @pl.when(me == r * stride)
        def _():
            for c in range(CHUNKS):
                for q in range(1, QUARTERS):
                    first(r, q, c).wait_send()

        @pl.when(plane == r * stride // QUARTERS)
        def _():
            for c in range(CHUNKS):
                for step in range(1, planes):
                    down(r, step, c).wait_send()

        for step in range(1, QUARTERS):
            @pl.when(neighbour(step) != r * stride)
            def _():
                for c in range(CHUNKS):
                    across(r, step, c).wait_send()


def share(row, count):
    planes = count // QUARTERS
    anywhere = pl.BlockSpec(memory_space=pl.ANY)
    dma = pltpu.SemaphoreType.DMA
    return pl.pallas_call(
        functools.partial(share_kernel, count),
        out_shape=jax.ShapeDtypeStruct((NP,) + row.shape, row.dtype),
        in_specs=[pl.BlockSpec(memory_space=pltpu.HBM)],
        out_specs=anywhere,
        scratch_shapes=[
            dma((QUARTERS - 1, CHUNKS)), dma((NP, planes - 1, CHUNKS)),
            dma((NP, QUARTERS - 1, CHUNKS)), dma((NP, QUARTERS, CHUNKS)), dma,
        ],
        compiler_params=pltpu.CompilerParams(
            collective_id=0, has_side_effects=True, vmem_limit_bytes=1 << 20
        ),
        name="share",
    )(row)


def sum_kernel(count, part, total, held, send, receive):
    me = lax.axis_index("band")
    barrier_all(me, count)

    def copy(step):
        return remote(part, held.at[step], send.at[step], receive.at[step],
                      lax.rem(me + step, count))

    for step in range(1, count):
        copy(step).start()
    held[0] = part[...]
    for step in range(1, count):
        copy(step).wait()
    total[...] = jnp.sum(held[...], axis=0)


def sum_all(part, count):
    vmem = pl.BlockSpec(memory_space=pltpu.VMEM)
    return pl.pallas_call(
        functools.partial(sum_kernel, count),
        out_shape=jax.ShapeDtypeStruct(part.shape, jnp.float32),
        in_specs=[vmem],
        out_specs=vmem,
        scratch_shapes=[
            pltpu.VMEM((count,) + part.shape, jnp.float32),
            pltpu.SemaphoreType.DMA((count,)),
            pltpu.SemaphoreType.DMA((count,)),
        ],
        compiler_params=pltpu.CompilerParams(
            collective_id=1, has_side_effects=True, vmem_limit_bytes=4 << 20
        ),
        name="sum_all",
    )(part)


def pick_kernel(orbitals, first, last):
    owned, width = orbitals.shape
    values = orbitals[...].astype(jnp.float32)
    first[...] = values[0:1].reshape(width // PAD, PAD).astype(first.dtype)
    last[...] = values[owned - 1 : owned].reshape(width // PAD, PAD).astype(last.dtype)


def pick(orbitals):
    owned, points = orbitals.shape
    steps = 10
    width = points // steps
    row = jax.ShapeDtypeStruct((points // PAD, PAD), orbitals.dtype)
    spec = pl.BlockSpec((width // PAD, PAD), lambda i: (i, 0))
    return pl.pallas_call(
        pick_kernel,
        grid=(steps,),
        out_shape=(row, row),
        in_specs=[pl.BlockSpec((owned, width), lambda i: (0, i))],
        out_specs=(spec, spec),
        compiler_params=pltpu.CompilerParams(vmem_limit_bytes=6 << 20),
        name="pick",
    )(orbitals)


def split(values):
    high = values.astype(jnp.bfloat16)
    low = (values - high.astype(jnp.float32)).astype(jnp.bfloat16)
    return high, low


def dot(left, right):
    return lax.dot_general(left, right, (((1,), (0,)), ((), ())),
                           preferred_element_type=jnp.float32)


def from_left(table, values):
    high, low = split(values)
    return dot(table, jnp.concatenate([high, low, high], axis=0))


def from_right(values, table):
    high, low = split(values)
    both = dot(high, table)
    return both[:, :PAD] + both[:, PAD:] + dot(low, table[:, :PAD])


def exchange_kernel(count, target_in, partners_in, forward_left, inverse_left, forward_right,
                    inverse_right, row_squares, lane_squares, slabs, vectors, gathered, one, two,
                    target, partners, done, send, receive, own_sem, load_sem, done_sem):
    group = 8
    me = lax.axis_index("band")
    loads = [
        pltpu.make_async_copy(target_in, target, load_sem.at[0]),
        pltpu.make_async_copy(partners_in, partners, load_sem.at[1]),
    ]
    for load in loads:
        load.start()
    barrier_all(me, count)

    def slab(step):
        other = lax.rem(me + step, count)
        return remote(slabs.at[other], gathered.at[me], send.at[step], receive.at[step], other)

    for step in range(1, count):
        slab(step).start()
    own = pltpu.make_async_copy(slabs.at[me], gathered.at[me], own_sem)
    own.start()
    for load in loads:
        load.wait()

    def ahead(step, carry):
        planes = pl.ds(step * group, group)
        left = target[planes].astype(jnp.float32)
        parts = []
        for r in range(NP):
            density = left * partners[r, planes].astype(jnp.float32)
            parts.append(from_right(density.reshape(group * NG, NG), forward_right[...]))
        values = jnp.concatenate(parts, axis=1).reshape(group, NG, NP * PAD)
        out = jnp.stack([from_left(forward_left[...], values[i]) for i in range(group)])
        one[:, pl.ds(pl.multiple_of(step * group, group), group), :] = jnp.swapaxes(out, 0, 1)
        return carry

    lax.fori_loop(0, NG // group, ahead, 0)

    def middle(step, carry):
        outs = []
        for i in range(group):
            number = step * group + i
            folded = jnp.where(number <= NG // 2, number, number - NG // 2)
            wave = (2.0 * np.pi / NG) * folded.astype(jnp.float32)
            totals = row_squares[...] + lane_squares[...] + wave * wave
            weight = jnp.where(totals > 0.0, 1.0 / (0.0025 + totals), 0.0)
            spectrum = from_left(forward_left[...], one[number]) * weight
            outs.append(from_left(inverse_left[...], spectrum))
        out = jnp.stack(outs)
        two[:, pl.ds(pl.multiple_of(step * group, group), group), :] = jnp.swapaxes(out, 0, 1)
        return carry

    lax.fori_loop(0, NG // group, middle, 0)

    def back(step, carry):
        planes = pl.ds(step * group, group)
        values = jnp.stack(
            [from_left(inverse_left[...], two[step * group + i]) for i in range(group)]
        ).reshape(group * NG, NP * PAD)
        total = jnp.zeros((group, NG, NG), jnp.float32)
        for r in range(NP):
            potential = from_right(values[:, r * PAD : (r + 1) * PAD], inverse_right[...])
            potential = potential.reshape(group, NG, PAD)[:, :, :NG]
            total -= partners[r, planes].astype(jnp.float32) * potential
        done[planes] = total
        stored(step).start()
        return carry

    def stored(step):
        planes = pl.ds(step * group, group)
        return pltpu.make_async_copy(done.at[planes], vectors.at[planes], done_sem.at[step])

    lax.fori_loop(0, NG // group, back, 0)
    for step in range(NG // group):
        stored(step).wait()
    own.wait()
    for step in range(1, count):
        slab(step).wait()


def exchange(target, partners, slabs, count):
    fourier, squares = tables(NG)
    lanes = np.zeros((PAD,), np.float32)
    lanes[:NG] = squares
    vmem = pl.BlockSpec(memory_space=pltpu.VMEM)
    anywhere = pl.BlockSpec(memory_space=pl.ANY)
    dma = pltpu.SemaphoreType.DMA
    return pl.pallas_call(
        functools.partial(exchange_kernel, count),
        out_shape=(
            jax.ShapeDtypeStruct((NG, NG, NG), jnp.float32),
            jax.ShapeDtypeStruct(slabs.shape, slabs.dtype),
        ),
        in_specs=[anywhere] * 2 + [vmem] * 6 + [anywhere],
        out_specs=(anywhere, anywhere),
        scratch_shapes=[pltpu.VMEM((NG, NG, NP * PAD), jnp.float32)] * 2
        + [
            pltpu.VMEM(target.shape, target.dtype),
            pltpu.VMEM(partners.shape, partners.dtype),
            pltpu.VMEM((NG, NG, NG), jnp.float32),
            dma((count,)), dma((count,)), dma, dma((2,)), dma((NG // 8,)),
        ],
        compiler_params=pltpu.CompilerParams(
            collective_id=2, has_side_effects=True, vmem_limit_bytes=60 << 20
        ),
        cost_estimate=pl.CostEstimate(
            flops=12 * NP * NG**4, bytes_accessed=8 << 20, transcendentals=0
        ),
        name="exchange",
    )(
        target,
        partners,
        left_table(fourier),
        left_table(fourier.T.copy()),
        right_table(fourier.T.copy(), NG),
        right_table(fourier, PAD),
        np.broadcast_to(squares[:, None], (NG, NP * PAD)).copy(),
        np.tile(lanes, NP)[None, :],
        slabs,
    )


TARGETS_AT = 7
LAG = 3
CHUNK = 125
GROUP = 8
WIDE = 32
HALF = 128
SPAN = 2 * HALF
PIECES = 32
STEPS = PIECES // QUARTERS


def chunks_kernel(orbitals, first, last):
    owned, width = orbitals.shape
    values = orbitals[...].astype(jnp.float32)
    size = CHUNK * PAD
    for i in range(width // size):
        piece = values[:, i * size : (i + 1) * size]
        for out, row in ((first, 0), (last, owned - 1)):
            value = piece[row : row + 1].reshape(CHUNK, PAD)
            value = jnp.concatenate([value, jnp.zeros((HALF - CHUNK, PAD), jnp.float32)], axis=0)
            out[i] = value.astype(out.dtype)


def chunks(orbitals):
    owned, points = orbitals.shape
    steps = 8
    row = jax.ShapeDtypeStruct((PIECES, HALF, PAD), orbitals.dtype)
    spec = pl.BlockSpec((PIECES // steps, HALF, PAD), lambda i: (i, 0, 0))
    return pl.pallas_call(
        chunks_kernel,
        grid=(steps,),
        out_shape=(row, row),
        in_specs=[pl.BlockSpec((owned, points // steps), lambda i: (0, i))],
        out_specs=(spec, spec),
        compiler_params=pltpu.CompilerParams(vmem_limit_bytes=8 << 20),
        name="chunks",
    )(orbitals)


def right_square(table):
    high, low = halves(table)
    rows, columns = table.shape
    result = np.zeros((2 * PAD, 2 * PAD), dtype=high.dtype)
    result[:rows, :columns] = high
    result[:rows, PAD : PAD + columns] = low
    result[PAD : PAD + rows, :columns] = high
    return result


def right(values, table):
    both = dot(jnp.concatenate(split(values), axis=1), table)
    return both[:, :PAD] + both[:, PAD:]


def flip(number, mask):
    result = number
    for bit in (1, 2, 4, 8):
        mine = lax.rem(lax.div(number, bit), 2)
        asked = lax.rem(lax.div(mask, bit), 2) if not isinstance(mask, int) else (mask // bit) % 2
        result = result + asked * (bit - 2 * bit * mine)
    return result


def spread(source, target, base):
    rows = [source[pl.ds(j, WIDE, stride=5), :] for j in range(5)]
    lane = lax.broadcasted_iota(jnp.int32, (WIDE, PAD), 1)
    for a in range(GROUP):
        row, offset = divmod(NG * a, PAD)
        value = rows[row]
        if offset + NG > PAD:
            value = jnp.where(lane >= offset, value, rows[row + 1])
        if offset:
            value = pltpu.roll(value, PAD - offset, 1)
        target[pl.ds(base + a, WIDE, stride=GROUP), :] = value


def gather(source, base, target):
    lane = lax.broadcasted_iota(jnp.int32, (WIDE, PAD), 1)
    rows = []
    for a in range(GROUP):
        value = source[pl.ds(base + a, WIDE, stride=GROUP), :]
        shift = NG * a % PAD
        rows.append(pltpu.roll(value, shift, 1) if shift else value)
    for j in range(5):
        low, high = PAD * j // NG, (PAD * j + PAD - 1) // NG
        value = rows[low]
        for a in range(low + 1, high + 1):
            value = jnp.where(lane >= NG * a - PAD * j, rows[a], value)
        target[pl.ds(j, WIDE, stride=5), :] = value


def flag(condition):
    return jnp.where(condition, 1, 0)


def vectors_kernel(count, targets_in, row_in, forward_left, inverse_left, forward_right,
                   inverse_right, row_squares, lane_squares, vectors, total,
                   one, two, part, landed, wide, target, partners, padded, outgoing, incoming,
                   points, products, sums,
                   part_send, part_receive, target_send, target_receive, vector_send,
                   vector_receive, sum_send, sum_receive, own_sem, out_sem):
    me = lax.axis_index("band")
    stride = count // NP
    layers = count // QUARTERS
    column = lax.rem(me, QUARTERS)
    layer = lax.div(me, QUARTERS)
    beside, behind = flip(me, 1), flip(me, 2)

    for r in range(NP):
        @pl.when(me == r * stride)
        def _():
            own = pltpu.make_async_copy(row_in, part.at[r], own_sem.at[0])
            own.start()
            own.wait()

    barrier_all(me, count)

    def slab_of_target(mask):
        other = flip(me, mask)
        return remote(targets_in.at[pl.ds(2 * other, 2)], landed.at[pl.ds(2 * me, 2)],
                      target_send.at[mask], target_receive.at[mask], other)

    def own_target():
        return pltpu.make_async_copy(targets_in.at[pl.ds(2 * me, 2)], landed.at[pl.ds(2 * me, 2)],
                                     own_sem.at[1])

    def forward(r, n, way, other):
        return remote(part.at[r, n], part.at[r, n], part_send.at[r, n, way],
                      part_receive.at[r, n], other)

    def own_ways(r):
        at_source = layer == r * stride // QUARTERS
        return [
            jnp.where(at_source, lax.rem(me + d * QUARTERS, count),
                      layer * QUARTERS + flip(column, d))
            for d in range(1, QUARTERS)
        ]

    def chain(q):
        ends = (column == 0) | (column == QUARTERS - 1)
        if q < 2:
            return ends | (column == 1), jnp.where(ends, beside, behind)
        return ends | (column == 2), jnp.where(ends, behind, beside)

    def start_all(r, c):
        for d, other in enumerate(own_ways(r)):
            forward(r, QUARTERS * c + column, d, other).start()

    def seed(r):
        def step(c, carry):
            start_all(r, c)
            for q in range(QUARTERS):
                forward(r, QUARTERS * c + q, 3, chain(q)[1]).start()
            return carry

        lax.fori_loop(0, STEPS, step, 0)

    for r in range(NP):
        @pl.when(me == r * stride)
        def _():
            seed(r)

    def wait_part(r, n):
        forward(r, n, 0, beside).wait_recv()

    def hand_on(r, i):
        at_source = layer == r * stride // QUARTERS
        c = i - flag(~at_source)

        @pl.when((c >= 0) & (c < STEPS) & (me != r * stride))
        def _():
            wait_part(r, QUARTERS * c + column)
            start_all(r, c)
            for q in (3, 1, 2, 0):
                @pl.when(at_source & chain(q)[0])
                def _():
                    @pl.when(column != q)
                    def _():
                        wait_part(r, QUARTERS * c + q)

                    forward(r, QUARTERS * c + q, 3, chain(q)[1]).start()

    def receive_rest(r, c):
        at_source = layer == r * stride // QUARTERS
        for q in range(QUARTERS):
            @pl.when((me != r * stride) & (column != q) & ~(at_source & chain(q)[0]))
            def _():
                wait_part(r, QUARTERS * c + q)

    def load(n, carry):
        wide[0:HALF] = targets_in[n].astype(jnp.float32)
        spread(wide, target, pl.multiple_of(n * 200, 8))
        return carry

    def ahead(step, carry):
        rows = pl.ds(pl.multiple_of(step * GROUP * NG, GROUP * NG), GROUP * NG)
        left = target[rows]
        parts = [right(left * partners[r, rows], forward_right[...]) for r in range(NP)]
        values = jnp.concatenate(parts, axis=1).reshape(GROUP, NG, NP * PAD)
        out = jnp.stack([from_left(forward_left[...], values[i]) for i in range(GROUP)])
        one[:, pl.ds(pl.multiple_of(step * GROUP, GROUP), GROUP), :] = jnp.swapaxes(out, 0, 1)
        return carry

    def relay(i, carry):
        for r in range(NP):
            hand_on(r, i)

        @pl.when(i == TARGETS_AT)
        def _():
            for mask in list(range(count // 2, count)) + list(range(1, count // 2)):
                slab_of_target(mask).start()
            own_target().start()

        @pl.when(i == 0)
        def _():
            lax.fori_loop(0, PIECES, load, 0)

        @pl.when(i >= LAG)
        def _():
            c = i - LAG
            for r in range(NP):
                receive_rest(r, c)

            def arrived(q, carry):
                n = c * QUARTERS + q
                for r in range(NP):
                    wide[0:HALF] = part[r, n].astype(jnp.float32)
                    spread(wide, partners.at[r], pl.multiple_of(n * 200, 8))
                return carry

            lax.fori_loop(0, QUARTERS, arrived, 0)
            lax.fori_loop(lax.div(10 * c, GROUP), lax.div(10 * (c + 1), GROUP), ahead, 0)

        return carry

    lax.fori_loop(0, STEPS + LAG, relay, 0)

    def middle(step, carry):
        outs = []
        for i in range(GROUP):
            number = step * GROUP + i
            folded = jnp.where(number <= NG // 2, number, number - NG // 2)
            wave = (2.0 * np.pi / NG) * folded.astype(jnp.float32)
            totals = row_squares[...] + lane_squares[...] + wave * wave
            weight = jnp.where(totals > 0.0, 1.0 / (0.0025 + totals), 0.0)
            spectrum = from_left(forward_left[...], one[number]) * weight
            outs.append(from_left(inverse_left[...], spectrum))
        out = jnp.stack(outs)
        two[:, pl.ds(pl.multiple_of(step * GROUP, GROUP), GROUP), :] = jnp.swapaxes(out, 0, 1)
        return carry

    lax.fori_loop(0, NG // GROUP, middle, 0)

    planes = NG // count
    padded[pl.ds(planes * NG, 64)] = jnp.zeros((64, PAD), jnp.float32)

    def slab(mask):
        other = flip(me, mask)
        return remote(outgoing.at[other, pl.ds(0, SPAN)], incoming.at[me], vector_send.at[mask],
                      vector_receive.at[mask], other)

    def own_slab():
        return pltpu.make_async_copy(outgoing.at[me, pl.ds(0, SPAN)], incoming.at[me],
                                     own_sem.at[0])

    def back(step, carry):
        mask = lax.rem(step + count // 2, count)
        s = flip(me, mask)
        values = jnp.concatenate(
            [from_left(inverse_left[...], two[s * planes + i]) for i in range(planes)], axis=0
        )
        rows = pl.ds(pl.multiple_of(s * planes * NG, planes * NG), planes * NG)
        result = jnp.zeros((planes * NG, PAD), jnp.float32)
        for r in range(NP):
            potential = right(values[:, r * PAD : (r + 1) * PAD], inverse_right[...])
            result -= partners[r, rows] * potential
        padded[0 : planes * NG] = result
        for h in range(2):
            gather(padded, h * 200, outgoing.at[s, pl.ds(h * HALF, 160)])

        @pl.when(mask != 0)
        def _():
            slab(mask).start()

        @pl.when(mask == 0)
        def _():
            own_slab().start()

        return carry

    lax.fori_loop(0, count, back, 0)

    own_target().wait()
    for mask in range(1, count):
        slab_of_target(mask).wait()

    def lift(n, carry):
        points[pl.ds(pl.multiple_of(n * HALF, HALF), HALF)] = landed[n].astype(jnp.float32)
        return carry

    lax.fori_loop(0, PIECES, lift, 0)

    def sent(c, carry):
        for r in range(NP):
            at_source = layer == r * stride // QUARTERS
            for d, other in enumerate(own_ways(r)):
                forward(r, QUARTERS * c + column, d, other).wait_send()
            for q in range(QUARTERS):
                wanted, other = chain(q)

                @pl.when(at_source & wanted)
                def _():
                    forward(r, QUARTERS * c + q, 3, other).wait_send()
        return carry

    lax.fori_loop(0, STEPS, sent, 0)

    def meet(mask, carry):
        @pl.when(mask != 0)
        def _():
            slab(mask).wait_recv()

        @pl.when(mask == 0)
        def _():
            own_slab().wait()

        b = flip(me, mask)
        values = incoming[b]
        for a in range(count):
            product = points[a * SPAN : (a + 1) * SPAN] * values
            product = jnp.sum(product.reshape(SPAN // 8, 8, PAD), axis=0)
            products[pl.ds(b * count + a, 1)] = jnp.sum(product, axis=0, keepdims=True)
        return carry

    lax.fori_loop(0, count, meet, 0)
    out = pltpu.make_async_copy(incoming, vectors, out_sem)
    out.start()

    line = jnp.sum(products[...], axis=1, keepdims=True)
    row = lax.broadcasted_iota(jnp.int32, (count * count, PAD), 0)
    lane = lax.broadcasted_iota(jnp.int32, (count * count, PAD), 1)
    placed = jnp.where(lane == lax.rem(row, count), line, 0.0)
    sums[me] = jnp.sum(placed.reshape(count, count, PAD), axis=1)

    def share_sum(mask):
        return remote(sums.at[me], sums.at[me], sum_send.at[mask], sum_receive.at[mask],
                      flip(me, mask))

    for mask in range(count - 1, 0, -1):
        share_sum(mask).start()
    for mask in range(1, count):
        slab(mask).wait_send()
    for mask in range(1, count):
        share_sum(mask).wait()
    total[...] = jnp.sum(sums[...], axis=0)
    out.wait()


def vectors_of(targets, row, count):
    fourier, squares = tables(NG)
    lanes = np.zeros((PAD,), np.float32)
    lanes[:NG] = squares
    vmem = pl.BlockSpec(memory_space=pltpu.VMEM)
    anywhere = pl.BlockSpec(memory_space=pl.ANY)
    dma = pltpu.SemaphoreType.DMA
    cube = NG * NG + 64
    planes = NG // count
    return pl.pallas_call(
        functools.partial(vectors_kernel, count),
        out_shape=(
            jax.ShapeDtypeStruct((count, SPAN, PAD), jnp.float32),
            jax.ShapeDtypeStruct((count, PAD), jnp.float32),
        ),
        in_specs=[vmem] * 8,
        out_specs=(anywhere, vmem),
        scratch_shapes=[
            pltpu.VMEM((NG, NG, NP * PAD), jnp.float32),
            pltpu.VMEM((NG, NG, NP * PAD), jnp.float32),
            pltpu.VMEM((NP, PIECES, HALF, PAD), row.dtype),
            pltpu.VMEM((PIECES, HALF, PAD), row.dtype),
            pltpu.VMEM((160, PAD), jnp.float32),
            pltpu.VMEM((cube, PAD), jnp.float32),
            pltpu.VMEM((NP, cube, PAD), jnp.float32),
            pltpu.VMEM((planes * NG + 64, PAD), jnp.float32),
            pltpu.VMEM((count, SPAN + 32, PAD), jnp.float32),
            pltpu.VMEM((count, SPAN, PAD), jnp.float32),
            pltpu.VMEM((count * SPAN, PAD), jnp.float32),
            pltpu.VMEM((count * count, PAD), jnp.float32),
            pltpu.VMEM((count, count, PAD), jnp.float32),
            dma((NP, PIECES, 4)), dma((NP, PIECES)), dma((count,)), dma((count,)),
            dma((count,)), dma((count,)), dma((count,)), dma((count,)), dma((2,)), dma,
        ],
        compiler_params=pltpu.CompilerParams(
            collective_id=3, has_side_effects=True, vmem_limit_bytes=50 << 20
        ),
        cost_estimate=pl.CostEstimate(
            flops=12 * NP * NG**4, bytes_accessed=8 << 20, transcendentals=0
        ),
        name="vectors",
    )(
        targets,
        row,
        left_table(fourier),
        left_table(fourier.T.copy()),
        right_square(fourier.T.copy()),
        right_square(fourier),
        np.broadcast_to(squares[:, None], (NG, NP * PAD)).copy(),
        np.tile(lanes, NP)[None, :],
    )


def finish_kernel(total, vectors, projector, factors, mixed):
    count = total.shape[0]
    scale = -0.5 / NG**3
    square = jnp.concatenate([total[...], jnp.zeros((PAD - count, PAD), jnp.float32)], axis=0)
    metric = scale * (square + square.T)[:count]
    row = lax.broadcasted_iota(jnp.int32, (count, PAD), 0)
    lane = lax.broadcasted_iota(jnp.int32, (count, PAD), 1)
    state = metric + jnp.where(lane == row + count, 1.0, 0.0)
    for k in range(count - 1):
        pivot = state[k : k + 1]
        ratio = state[:, k : k + 1] / pivot[:, k : k + 1]
        state = state - jnp.where(row > k, ratio, 0.0) * pivot
    diagonal = jnp.sum(jnp.where(lane == row, state, 0.0), axis=1, keepdims=True)
    state = state * (1.0 / jnp.sqrt(diagonal))
    for j in range(count):
        factors[j] = jnp.broadcast_to(state[:, count + j : count + j + 1], (count, PAD))

    size = 32

    def mix(step, carry):
        rows = pl.ds(pl.multiple_of(step * size, size), size)
        values = [vectors[j, rows] for j in range(count)]
        for k in range(count):
            result = factors[0, k : k + 1] * values[0]
            for j in range(1, k + 1):
                result += factors[j, k : k + 1] * values[j]
            mixed[pl.ds(step * size * count + k, size, stride=count), :] = result
        return carry

    lax.fori_loop(0, SPAN // size, mix, 0)

    unroll = 25

    def write(step, carry):
        for h in range(2):
            for i in range(unroll):
                rows = pl.ds(pl.multiple_of((h * HALF + step * unroll + i) * count, count), count)
                start = pl.multiple_of((h * CHUNK + step * unroll + i) * PAD, PAD)
                projector[:, pl.ds(start, PAD)] = mixed[rows]
        return carry

    lax.fori_loop(0, CHUNK // unroll, write, 0)


def finish(total, vectors):
    count = total.shape[0]
    vmem = pl.BlockSpec(memory_space=pltpu.VMEM)
    return pl.pallas_call(
        finish_kernel,
        out_shape=jax.ShapeDtypeStruct((count, 2 * CHUNK * PAD), jnp.float32),
        in_specs=[vmem, vmem],
        out_specs=vmem,
        scratch_shapes=[
            pltpu.VMEM((count, count, PAD), jnp.float32),
            pltpu.VMEM((SPAN * count, PAD), jnp.float32),
        ],
        compiler_params=pltpu.CompilerParams(vmem_limit_bytes=16 << 20),
        name="finish",
    )(total, vectors)


def fast_body(orbitals):
    targets, row = chunks(orbitals)
    vectors, total = vectors_of(targets, row, lax.axis_size("band"))
    return finish(total, vectors)


def body(orbitals):
    devices = lax.axis_size("band")
    points = orbitals.shape[1]
    target, row = pick(orbitals)
    partners = share(row.reshape(QUARTERS, CHUNKS, -1, PAD), devices)
    vectors, target_slab = exchange(
        target.reshape(NG, NG, NG),
        partners.reshape(NP, NG, NG, NG),
        target.reshape(devices, 8, points // devices // 8),
        devices,
    )
    vector_slab = lax.all_to_all(
        vectors.reshape(1, points), "band", split_axis=1, concat_axis=0, tiled=True
    )
    target_slab = target_slab.reshape(devices, points // devices).astype(jnp.float32)
    part = jnp.einsum("ap,bp->ab", target_slab, vector_slab, precision=highest) / NG**3
    intersection = sum_all(part, devices)
    metric = -0.5 * (intersection + intersection.T)
    factor = lax.linalg.cholesky(metric, symmetrize_input=False)
    return jax.scipy.linalg.solve_triangular(factor, vector_slab, lower=True)


def solution(mesh):
    placed = (P(("spin", "band"), None),)
    fast = mesh.shape["band"] == 2 * NP * QUARTERS
    return jax.shard_map(
        fast_body if fast else body, mesh=mesh, in_specs=placed, out_specs=P("spin", "band"), check_vma=False
    )
```

```python
import functools

import jax
import jax.numpy as jnp
import numpy as np
from jax import lax
from jax.experimental import pallas as pl
from jax.experimental.pallas import tpu as pltpu
from jax.sharding import PartitionSpec as P

NG = 80
NP = 2
PAD = 128
QUARTERS = 4
CHUNKS = 5
highest = lax.Precision.HIGHEST


def tables(length):
    indices = np.arange(length)
    nyquist = length // 2
    frequency = np.where(indices <= nyquist, indices, indices - nyquist)
    angles = 2.0 * np.pi / length * (frequency[:, None] * indices[None, :] % length)
    edges = (indices == 0) | (indices == nyquist)
    weights = np.where(edges, 1.0 / length, 2.0 / length)
    fourier = np.where((indices <= nyquist)[:, None], np.cos(angles), np.sin(angles))
    fourier = (fourier * np.sqrt(weights)[:, None]).astype(np.float32)
    squares = ((2.0 * np.pi / length * frequency) ** 2).astype(np.float32)
    return fourier, squares


def halves(table):
    high = table.astype(jnp.bfloat16)
    low = (table - high.astype(np.float32)).astype(jnp.bfloat16)
    return high, low


def left_table(table):
    high, low = halves(table)
    return np.concatenate([high, high, low], axis=1)


def right_table(table, depth):
    high, low = halves(table)
    result = np.zeros((depth, 2 * PAD), dtype=high.dtype)
    result[: table.shape[0], : table.shape[1]] = high
    result[: table.shape[0], PAD : PAD + table.shape[1]] = low
    return result


def barrier_all(me, count):
    barrier = pltpu.get_barrier_semaphore()
    for step in range(1, count):
        pl.semaphore_signal(
            barrier, inc=1, device_id={"band": lax.rem(me + step, count)},
            device_id_type=pl.DeviceIdType.MESH,
        )
    pl.semaphore_wait(barrier, count - 1)


def remote(source, target, send, receive, device):
    return pltpu.make_async_remote_copy(
        src_ref=source, dst_ref=target, send_sem=send, recv_sem=receive,
        device_id={"band": device}, device_id_type=pl.DeviceIdType.MESH,
    )


def share_kernel(count, row, partners, first_send, column_send, plane_send, receive, own_sem):
    me = lax.axis_index("band")
    planes = count // QUARTERS
    stride = count // NP
    column = lax.rem(me, QUARTERS)
    plane = lax.div(me, QUARTERS)
    base = plane * QUARTERS
    barrier_all(me, count)

    def first(r, q, c):
        return remote(row.at[q, c], partners.at[r, q, c], first_send.at[q - 1, c],
                      receive.at[r, q, c], lax.rem(me + q, count))

    def down(r, step, c):
        other = lax.rem(me + step * QUARTERS, count)
        return remote(partners.at[r, column, c], partners.at[r, column, c],
                      column_send.at[r, step - 1, c], receive.at[r, column, c], other)

    def neighbour(step):
        return base + lax.rem(column + step, QUARTERS)

    def across(r, step, c):
        return remote(partners.at[r, column, c], partners.at[r, column, c],
                      plane_send.at[r, step - 1, c], receive.at[r, column, c], neighbour(step))

    def arrived(r, q, c):
        remote(partners.at[r, q, c], partners.at[r, q, c], plane_send.at[r, 0, c],
               receive.at[r, q, c], me).wait_recv()

    for r in range(NP):
        @pl.when(me == r * stride)
        def _():
            own = pltpu.make_async_copy(row, partners.at[r], own_sem)
            own.start()
            own.wait()

    for c in range(CHUNKS):
        for r in range(NP):
            @pl.when(me != r * stride)
            def _():
                arrived(r, column, c)

            @pl.when(me == r * stride)
            def _():
                for q in range(1, QUARTERS):
                    first(r, q, c).start()

            @pl.when(plane == r * stride // QUARTERS)
            def _():
                for step in range(1, planes):
                    down(r, step, c).start()

            for step in range(1, QUARTERS):
                @pl.when(neighbour(step) != r * stride)
                def _():
                    across(r, step, c).start()

    for r in range(NP):
        @pl.when(me != r * stride)
        def _():
            for c in range(CHUNKS):
                for step in range(1, QUARTERS):
                    arrived(r, lax.rem(column + step, QUARTERS), c)

        @pl.when(me == r * stride)
        def _():
            for c in range(CHUNKS):
                for q in range(1, QUARTERS):
                    first(r, q, c).wait_send()

        @pl.when(plane == r * stride // QUARTERS)
        def _():
            for c in range(CHUNKS):
                for step in range(1, planes):
                    down(r, step, c).wait_send()

        for step in range(1, QUARTERS):
            @pl.when(neighbour(step) != r * stride)
            def _():
                for c in range(CHUNKS):
                    across(r, step, c).wait_send()


def share(row, count):
    planes = count // QUARTERS
    anywhere = pl.BlockSpec(memory_space=pl.ANY)
    dma = pltpu.SemaphoreType.DMA
    return pl.pallas_call(
        functools.partial(share_kernel, count),
        out_shape=jax.ShapeDtypeStruct((NP,) + row.shape, row.dtype),
        in_specs=[pl.BlockSpec(memory_space=pltpu.HBM)],
        out_specs=anywhere,
        scratch_shapes=[
            dma((QUARTERS - 1, CHUNKS)), dma((NP, planes - 1, CHUNKS)),
            dma((NP, QUARTERS - 1, CHUNKS)), dma((NP, QUARTERS, CHUNKS)), dma,
        ],
        compiler_params=pltpu.CompilerParams(
            collective_id=0, has_side_effects=True, vmem_limit_bytes=1 << 20
        ),
        name="share",
    )(row)


def sum_kernel(count, part, total, held, send, receive):
    me = lax.axis_index("band")
    barrier_all(me, count)

    def copy(step):
        return remote(part, held.at[step], send.at[step], receive.at[step],
                      lax.rem(me + step, count))

    for step in range(1, count):
        copy(step).start()
    held[0] = part[...]
    for step in range(1, count):
        copy(step).wait()
    total[...] = jnp.sum(held[...], axis=0)


def sum_all(part, count):
    vmem = pl.BlockSpec(memory_space=pltpu.VMEM)
    return pl.pallas_call(
        functools.partial(sum_kernel, count),
        out_shape=jax.ShapeDtypeStruct(part.shape, jnp.float32),
        in_specs=[vmem],
        out_specs=vmem,
        scratch_shapes=[
            pltpu.VMEM((count,) + part.shape, jnp.float32),
            pltpu.SemaphoreType.DMA((count,)),
            pltpu.SemaphoreType.DMA((count,)),
        ],
        compiler_params=pltpu.CompilerParams(
            collective_id=1, has_side_effects=True, vmem_limit_bytes=4 << 20
        ),
        name="sum_all",
    )(part)


def pick_kernel(orbitals, first, last):
    owned, width = orbitals.shape
    values = orbitals[...].astype(jnp.float32)
    first[...] = values[0:1].reshape(width // PAD, PAD).astype(first.dtype)
    last[...] = values[owned - 1 : owned].reshape(width // PAD, PAD).astype(last.dtype)


def pick(orbitals):
    owned, points = orbitals.shape
    steps = 10
    width = points // steps
    row = jax.ShapeDtypeStruct((points // PAD, PAD), orbitals.dtype)
    spec = pl.BlockSpec((width // PAD, PAD), lambda i: (i, 0))
    return pl.pallas_call(
        pick_kernel,
        grid=(steps,),
        out_shape=(row, row),
        in_specs=[pl.BlockSpec((owned, width), lambda i: (0, i))],
        out_specs=(spec, spec),
        compiler_params=pltpu.CompilerParams(vmem_limit_bytes=6 << 20),
        name="pick",
    )(orbitals)


def split(values):
    high = values.astype(jnp.bfloat16)
    low = (values - high.astype(jnp.float32)).astype(jnp.bfloat16)
    return high, low


def dot(left, right):
    return lax.dot_general(left, right, (((1,), (0,)), ((), ())),
                           preferred_element_type=jnp.float32)


def from_left(table, values):
    high, low = split(values)
    return dot(table, jnp.concatenate([high, low, high], axis=0))


def from_right(values, table):
    high, low = split(values)
    both = dot(high, table)
    return both[:, :PAD] + both[:, PAD:] + dot(low, table[:, :PAD])


def exchange_kernel(count, target_in, partners_in, forward_left, inverse_left, forward_right,
                    inverse_right, row_squares, lane_squares, slabs, vectors, gathered, one, two,
                    target, partners, done, send, receive, own_sem, load_sem, done_sem):
    group = 8
    me = lax.axis_index("band")
    loads = [
        pltpu.make_async_copy(target_in, target, load_sem.at[0]),
        pltpu.make_async_copy(partners_in, partners, load_sem.at[1]),
    ]
    for load in loads:
        load.start()
    barrier_all(me, count)

    def slab(step):
        other = lax.rem(me + step, count)
        return remote(slabs.at[other], gathered.at[me], send.at[step], receive.at[step], other)

    for step in range(1, count):
        slab(step).start()
    own = pltpu.make_async_copy(slabs.at[me], gathered.at[me], own_sem)
    own.start()
    for load in loads:
        load.wait()

    def ahead(step, carry):
        planes = pl.ds(step * group, group)
        left = target[planes].astype(jnp.float32)
        parts = []
        for r in range(NP):
            density = left * partners[r, planes].astype(jnp.float32)
            parts.append(from_right(density.reshape(group * NG, NG), forward_right[...]))
        values = jnp.concatenate(parts, axis=1).reshape(group, NG, NP * PAD)
        out = jnp.stack([from_left(forward_left[...], values[i]) for i in range(group)])
        one[:, pl.ds(pl.multiple_of(step * group, group), group), :] = jnp.swapaxes(out, 0, 1)
        return carry

    lax.fori_loop(0, NG // group, ahead, 0)

    def middle(step, carry):
        outs = []
        for i in range(group):
            number = step * group + i
            folded = jnp.where(number <= NG // 2, number, number - NG // 2)
            wave = (2.0 * np.pi / NG) * folded.astype(jnp.float32)
            totals = row_squares[...] + lane_squares[...] + wave * wave
            weight = jnp.where(totals > 0.0, 1.0 / (0.0025 + totals), 0.0)
            spectrum = from_left(forward_left[...], one[number]) * weight
            outs.append(from_left(inverse_left[...], spectrum))
        out = jnp.stack(outs)
        two[:, pl.ds(pl.multiple_of(step * group, group), group), :] = jnp.swapaxes(out, 0, 1)
        return carry

    lax.fori_loop(0, NG // group, middle, 0)

    def back(step, carry):
        planes = pl.ds(step * group, group)
        values = jnp.stack(
            [from_left(inverse_left[...], two[step * group + i]) for i in range(group)]
        ).reshape(group * NG, NP * PAD)
        total = jnp.zeros((group, NG, NG), jnp.float32)
        for r in range(NP):
            potential = from_right(values[:, r * PAD : (r + 1) * PAD], inverse_right[...])
            potential = potential.reshape(group, NG, PAD)[:, :, :NG]
            total -= partners[r, planes].astype(jnp.float32) * potential
        done[planes] = total
        stored(step).start()
        return carry

    def stored(step):
        planes = pl.ds(step * group, group)
        return pltpu.make_async_copy(done.at[planes], vectors.at[planes], done_sem.at[step])

    lax.fori_loop(0, NG // group, back, 0)
    for step in range(NG // group):
        stored(step).wait()
    own.wait()
    for step in range(1, count):
        slab(step).wait()


def exchange(target, partners, slabs, count):
    fourier, squares = tables(NG)
    lanes = np.zeros((PAD,), np.float32)
    lanes[:NG] = squares
    vmem = pl.BlockSpec(memory_space=pltpu.VMEM)
    anywhere = pl.BlockSpec(memory_space=pl.ANY)
    dma = pltpu.SemaphoreType.DMA
    return pl.pallas_call(
        functools.partial(exchange_kernel, count),
        out_shape=(
            jax.ShapeDtypeStruct((NG, NG, NG), jnp.float32),
            jax.ShapeDtypeStruct(slabs.shape, slabs.dtype),
        ),
        in_specs=[anywhere] * 2 + [vmem] * 6 + [anywhere],
        out_specs=(anywhere, anywhere),
        scratch_shapes=[pltpu.VMEM((NG, NG, NP * PAD), jnp.float32)] * 2
        + [
            pltpu.VMEM(target.shape, target.dtype),
            pltpu.VMEM(partners.shape, partners.dtype),
            pltpu.VMEM((NG, NG, NG), jnp.float32),
            dma((count,)), dma((count,)), dma, dma((2,)), dma((NG // 8,)),
        ],
        compiler_params=pltpu.CompilerParams(
            collective_id=2, has_side_effects=True, vmem_limit_bytes=60 << 20
        ),
        cost_estimate=pl.CostEstimate(
            flops=12 * NP * NG**4, bytes_accessed=8 << 20, transcendentals=0
        ),
        name="exchange",
    )(
        target,
        partners,
        left_table(fourier),
        left_table(fourier.T.copy()),
        right_table(fourier.T.copy(), NG),
        right_table(fourier, PAD),
        np.broadcast_to(squares[:, None], (NG, NP * PAD)).copy(),
        np.tile(lanes, NP)[None, :],
        slabs,
    )


TARGETS_AT = 7
LAG = 3
LEVELS = 240
CHUNK = 125
GROUP = 8
WIDE = 32
HALF = 128
SPAN = 2 * HALF
PIECES = 32
STEPS = PIECES // QUARTERS


def chunks_kernel(orbitals, first, last):
    owned, width = orbitals.shape
    values = orbitals[...].astype(jnp.float32)
    size = CHUNK * PAD
    for i in range(width // size):
        piece = values[:, i * size : (i + 1) * size]
        for out, row in ((first, 0), (last, owned - 1)):
            value = piece[row : row + 1].reshape(CHUNK, PAD)
            value = jnp.concatenate([value, jnp.zeros((HALF - CHUNK, PAD), jnp.float32)], axis=0)
            out[i] = value.astype(out.dtype)


def chunks(orbitals):
    owned, points = orbitals.shape
    steps = 8
    row = jax.ShapeDtypeStruct((PIECES, HALF, PAD), orbitals.dtype)
    spec = pl.BlockSpec((PIECES // steps, HALF, PAD), lambda i: (i, 0, 0))
    return pl.pallas_call(
        chunks_kernel,
        grid=(steps,),
        out_shape=(row, row),
        in_specs=[pl.BlockSpec((owned, points // steps), lambda i: (0, i))],
        out_specs=(spec, spec),
        compiler_params=pltpu.CompilerParams(vmem_limit_bytes=8 << 20),
        name="chunks",
    )(orbitals)


def right_square(table):
    high, low = halves(table)
    rows, columns = table.shape
    result = np.zeros((2 * PAD, 2 * PAD), dtype=high.dtype)
    result[:rows, :columns] = high
    result[:rows, PAD : PAD + columns] = low
    result[PAD : PAD + rows, :columns] = high
    return result


def right(values, table):
    both = dot(jnp.concatenate(split(values), axis=1), table)
    return both[:, :PAD] + both[:, PAD:]


def flip(number, mask):
    result = number
    for bit in (1, 2, 4, 8):
        mine = lax.rem(lax.div(number, bit), 2)
        asked = lax.rem(lax.div(mask, bit), 2) if not isinstance(mask, int) else (mask // bit) % 2
        result = result + asked * (bit - 2 * bit * mine)
    return result


def spread(source, target, base):
    rows = [source[pl.ds(j, WIDE, stride=5), :] for j in range(5)]
    lane = lax.broadcasted_iota(jnp.int32, (WIDE, PAD), 1)
    for a in range(GROUP):
        row, offset = divmod(NG * a, PAD)
        value = rows[row]
        if offset + NG > PAD:
            value = jnp.where(lane >= offset, value, rows[row + 1])
        if offset:
            value = pltpu.roll(value, PAD - offset, 1)
        target[pl.ds(base + a, WIDE, stride=GROUP), :] = value


def gather(source, base, target):
    lane = lax.broadcasted_iota(jnp.int32, (WIDE, PAD), 1)
    rows = []
    for a in range(GROUP):
        value = source[pl.ds(base + a, WIDE, stride=GROUP), :]
        shift = NG * a % PAD
        rows.append(pltpu.roll(value, shift, 1) if shift else value)
    for j in range(5):
        low, high = PAD * j // NG, (PAD * j + PAD - 1) // NG
        value = rows[low]
        for a in range(low + 1, high + 1):
            value = jnp.where(lane >= NG * a - PAD * j, rows[a], value)
        target[pl.ds(j, WIDE, stride=5), :] = value


def flag(condition):
    return jnp.where(condition, 1, 0)


def encode(values, inverse):
    level = jnp.sqrt(jnp.abs(values) * inverse) * LEVELS
    whole = jnp.floor(level)
    code = jnp.exp2(whole - LEVELS / 2) * (1.0 + (level - whole))
    return jnp.where(values < 0.0, -code, code)


def decode(codes, scale):
    size = jnp.maximum(jnp.abs(codes), 2.0 ** (-LEVELS / 2))
    whole = jnp.floor(jnp.log2(size))
    level = (whole + (LEVELS / 2 - 1.0) + size * jnp.exp2(-whole)) * (1.0 / LEVELS)
    level = level * level * scale
    return jnp.where(codes < 0.0, -level, level)


def vectors_kernel(count, targets_in, row_in, forward_left, inverse_left, forward_right,
                   inverse_right, row_squares, lane_squares, vectors, total,
                   one, two, part, landed, wide, target, partners, padded, flat, outgoing, incoming,
                   own_partners, decoded, points, products, sums,
                   part_send, part_receive, target_send, target_receive, vector_send,
                   vector_receive, sum_send, sum_receive, own_sem, out_sem):
    me = lax.axis_index("band")
    stride = count // NP
    layers = count // QUARTERS
    column = lax.rem(me, QUARTERS)
    layer = lax.div(me, QUARTERS)
    beside, behind = flip(me, 1), flip(me, 2)

    for r in range(NP):
        @pl.when(me == r * stride)
        def _():
            own = pltpu.make_async_copy(row_in, part.at[r], own_sem.at[0])
            own.start()
            own.wait()

    barrier_all(me, count)

    def slab_of_target(mask):
        other = flip(me, mask)
        return remote(targets_in.at[pl.ds(2 * other, 2)], landed.at[pl.ds(2 * me, 2)],
                      target_send.at[mask], target_receive.at[mask], other)

    def own_target():
        return pltpu.make_async_copy(targets_in.at[pl.ds(2 * me, 2)], landed.at[pl.ds(2 * me, 2)],
                                     own_sem.at[1])

    def forward(r, n, way, other):
        return remote(part.at[r, n], part.at[r, n], part_send.at[r, n, way],
                      part_receive.at[r, n], other)

    def own_ways(r):
        at_source = layer == r * stride // QUARTERS
        return [
            jnp.where(at_source, lax.rem(me + d * QUARTERS, count),
                      layer * QUARTERS + flip(column, d))
            for d in range(1, QUARTERS)
        ]

    def chain(q):
        ends = (column == 0) | (column == QUARTERS - 1)
        if q < 2:
            return ends | (column == 1), jnp.where(ends, beside, behind)
        return ends | (column == 2), jnp.where(ends, behind, beside)

    def start_all(r, c):
        for d, other in enumerate(own_ways(r)):
            forward(r, QUARTERS * c + column, d, other).start()

    def seed(r):
        def step(c, carry):
            start_all(r, c)
            for q in range(QUARTERS):
                forward(r, QUARTERS * c + q, 3, chain(q)[1]).start()
            return carry

        lax.fori_loop(0, STEPS, step, 0)

    for r in range(NP):
        @pl.when(me == r * stride)
        def _():
            seed(r)

    def wait_part(r, n):
        forward(r, n, 0, beside).wait_recv()

    def hand_on(r, i):
        at_source = layer == r * stride // QUARTERS
        c = i - flag(~at_source)

        @pl.when((c >= 0) & (c < STEPS) & (me != r * stride))
        def _():
            wait_part(r, QUARTERS * c + column)
            start_all(r, c)
            for q in (3, 1, 2, 0):
                @pl.when(at_source & chain(q)[0])
                def _():
                    @pl.when(column != q)
                    def _():
                        wait_part(r, QUARTERS * c + q)

                    forward(r, QUARTERS * c + q, 3, chain(q)[1]).start()

    def receive_rest(r, c):
        at_source = layer == r * stride // QUARTERS
        for q in range(QUARTERS):
            @pl.when((me != r * stride) & (column != q) & ~(at_source & chain(q)[0]))
            def _():
                wait_part(r, QUARTERS * c + q)

    def load(n, carry):
        wide[0:HALF] = targets_in[n].astype(jnp.float32)
        spread(wide, target, pl.multiple_of(n * 200, 8))
        return carry

    def ahead(step, carry):
        rows = pl.ds(pl.multiple_of(step * GROUP * NG, GROUP * NG), GROUP * NG)
        left = target[rows]
        parts = [right(left * partners[r, rows], forward_right[...]) for r in range(NP)]
        values = jnp.concatenate(parts, axis=1).reshape(GROUP, NG, NP * PAD)
        out = jnp.stack([from_left(forward_left[...], values[i]) for i in range(GROUP)])
        one[:, pl.ds(pl.multiple_of(step * GROUP, GROUP), GROUP), :] = jnp.swapaxes(out, 0, 1)
        return carry

    def relay(i, carry):
        for r in range(NP):
            hand_on(r, i)

        @pl.when(i == TARGETS_AT)
        def _():
            for mask in list(range(count // 2, count)) + list(range(1, count // 2)):
                slab_of_target(mask).start()
            own_target().start()

        @pl.when(i == 0)
        def _():
            lax.fori_loop(0, PIECES, load, 0)

        @pl.when(i >= LAG)
        def _():
            c = i - LAG
            for r in range(NP):
                receive_rest(r, c)

            def arrived(q, carry):
                n = c * QUARTERS + q
                for r in range(NP):
                    wide[0:HALF] = part[r, n].astype(jnp.float32)
                    spread(wide, partners.at[r], pl.multiple_of(n * 200, 8))
                return carry

            lax.fori_loop(0, QUARTERS, arrived, 0)
            lax.fori_loop(lax.div(10 * c, GROUP), lax.div(10 * (c + 1), GROUP), ahead, 0)

        return carry

    lax.fori_loop(0, STEPS + LAG, relay, 0)

    def middle(step, carry):
        outs = []
        for i in range(GROUP):
            number = step * GROUP + i
            folded = jnp.where(number <= NG // 2, number, number - NG // 2)
            wave = (2.0 * np.pi / NG) * folded.astype(jnp.float32)
            totals = row_squares[...] + lane_squares[...] + wave * wave
            weight = jnp.where(totals > 0.0, 1.0 / (0.0025 + totals), 0.0)
            spectrum = from_left(forward_left[...], one[number]) * weight
            outs.append(from_left(inverse_left[...], spectrum))
        out = jnp.stack(outs)
        two[:, pl.ds(pl.multiple_of(step * GROUP, GROUP), GROUP), :] = jnp.swapaxes(out, 0, 1)
        return carry

    lax.fori_loop(0, NG // GROUP, middle, 0)

    planes = NG // count
    padded[pl.ds(planes * NG, 64)] = jnp.zeros((64, PAD), jnp.float32)

    def slab(mask):
        other = flip(me, mask)
        return remote(outgoing.at[other], incoming.at[me], vector_send.at[mask],
                      vector_receive.at[mask], other)

    def own_slab():
        return pltpu.make_async_copy(outgoing.at[me], incoming.at[me],
                                     own_sem.at[0])

    def back(step, carry):
        mask = lax.rem(step + count // 2, count)
        s = flip(me, mask)
        spectra = [two[s * planes + i] for i in range(planes)]
        side = jnp.zeros((1, PAD), jnp.float32)
        lane = lax.broadcasted_iota(jnp.int32, (1, PAD), 1)
        for i in range(planes):
            for r in range(NP):
                mean = spectra[i][0:1, r * PAD : r * PAD + 1] / NG
                side = jnp.where(lane == 8 * r + i, mean, side)
        row = lax.broadcasted_iota(jnp.int32, (NG, NP * PAD), 0)
        column = lax.broadcasted_iota(jnp.int32, (NG, NP * PAD), 1)
        keep = (row != 0) | ((column != 0) & (column != PAD))
        values = jnp.concatenate(
            [from_left(inverse_left[...], jnp.where(keep, x, 0.0)) for x in spectra], axis=0
        )
        rows = pl.ds(pl.multiple_of(s * planes * NG, planes * NG), planes * NG)
        result = jnp.zeros((planes * NG, PAD), jnp.float32)
        for r in range(NP):
            potential = right(values[:, r * PAD : (r + 1) * PAD], inverse_right[...])
            result -= partners[r, rows] * potential
        padded[0 : planes * NG] = result
        for h in range(2):
            gather(padded, h * 200, flat.at[pl.ds(h * HALF, 160)])
        biggest = jnp.max(jnp.abs(result), axis=0, keepdims=True)
        biggest = jnp.max(biggest, axis=1, keepdims=True)
        side = jnp.where(lane == 16, biggest, side)
        inverse = jnp.where(biggest > 0.0, 1.0 / biggest, 0.0)
        codes = encode(flat[0:SPAN], inverse)
        high = side.astype(jnp.bfloat16).astype(jnp.float32)
        rest = side - high
        middling = rest.astype(jnp.bfloat16).astype(jnp.float32)
        line = lax.broadcasted_iota(jnp.int32, (8, PAD), 0)
        last = codes[HALF - 8 : HALF]
        for i, value in ((CHUNK, high), (CHUNK + 1, middling), (CHUNK + 2, rest - middling)):
            last = jnp.where(line == i - HALF + 8, value, last)
        codes = jnp.concatenate([codes[: HALF - 8], last, codes[HALF:]], axis=0)
        outgoing[s] = codes.astype(outgoing.dtype)

        @pl.when(mask != 0)
        def _():
            slab(mask).start()

        @pl.when(mask == 0)
        def _():
            own_slab().start()

        return carry

    lax.fori_loop(0, count, back, 0)

    own_target().wait()
    for mask in range(1, count):
        slab_of_target(mask).wait()

    def lift(n, carry):
        points[pl.ds(pl.multiple_of(n * HALF, HALF), HALF)] = landed[n].astype(jnp.float32)
        return carry

    lax.fori_loop(0, PIECES, lift, 0)

    def sent(c, carry):
        for r in range(NP):
            at_source = layer == r * stride // QUARTERS
            for d, other in enumerate(own_ways(r)):
                forward(r, QUARTERS * c + column, d, other).wait_send()
            for q in range(QUARTERS):
                wanted, other = chain(q)

                @pl.when(at_source & wanted)
                def _():
                    forward(r, QUARTERS * c + q, 3, other).wait_send()
        return carry

    lax.fori_loop(0, STEPS, sent, 0)

    for r in range(NP):
        for h in range(2):
            own_partners[r, h * HALF : (h + 1) * HALF] = part[r, 2 * me + h].astype(jnp.float32)
    line = lax.broadcasted_iota(jnp.int32, (SPAN, PAD), 0)
    plane = lax.div(line - flag(line >= HALF) * (HALF - CHUNK), NG * NG // PAD)

    def meet(mask, carry):
        @pl.when(mask != 0)
        def _():
            slab(mask).wait_recv()

        @pl.when(mask == 0)
        def _():
            own_slab().wait()

        b = flip(me, mask)
        codes = incoming[b].astype(jnp.float32)
        side = jnp.sum(codes[CHUNK:HALF], axis=0, keepdims=True)
        values = decode(codes, side[:, 16:17])
        for r in range(NP):
            mean = side[:, 8 * r : 8 * r + 1]
            for i in range(1, planes):
                mean = jnp.where(plane >= i, side[:, 8 * r + i : 8 * r + i + 1], mean)
            values -= own_partners[r] * mean
        decoded[b] = values
        for a in range(count):
            product = points[a * SPAN : (a + 1) * SPAN] * values
            product = jnp.sum(product.reshape(SPAN // 8, 8, PAD), axis=0)
            products[pl.ds(b * count + a, 1)] = jnp.sum(product, axis=0, keepdims=True)
        return carry

    lax.fori_loop(0, count, meet, 0)
    out = pltpu.make_async_copy(decoded, vectors, out_sem)
    out.start()

    line = jnp.sum(products[...], axis=1, keepdims=True)
    row = lax.broadcasted_iota(jnp.int32, (count * count, PAD), 0)
    lane = lax.broadcasted_iota(jnp.int32, (count * count, PAD), 1)
    placed = jnp.where(lane == lax.rem(row, count), line, 0.0)
    sums[me] = jnp.sum(placed.reshape(count, count, PAD), axis=1)

    def share_sum(mask):
        return remote(sums.at[me], sums.at[me], sum_send.at[mask], sum_receive.at[mask],
                      flip(me, mask))

    for mask in range(count - 1, 0, -1):
        share_sum(mask).start()
    for mask in range(1, count):
        slab(mask).wait_send()
    for mask in range(1, count):
        share_sum(mask).wait()
    total[...] = jnp.sum(sums[...], axis=0)
    out.wait()


def vectors_of(targets, row, count):
    fourier, squares = tables(NG)
    lanes = np.zeros((PAD,), np.float32)
    lanes[:NG] = squares
    vmem = pl.BlockSpec(memory_space=pltpu.VMEM)
    anywhere = pl.BlockSpec(memory_space=pl.ANY)
    dma = pltpu.SemaphoreType.DMA
    cube = NG * NG + 64
    planes = NG // count
    return pl.pallas_call(
        functools.partial(vectors_kernel, count),
        out_shape=(
            jax.ShapeDtypeStruct((count, SPAN, PAD), jnp.float32),
            jax.ShapeDtypeStruct((count, PAD), jnp.float32),
        ),
        in_specs=[vmem] * 8,
        out_specs=(anywhere, vmem),
        scratch_shapes=[
            pltpu.VMEM((NG, NG, NP * PAD), jnp.float32),
            pltpu.VMEM((NG, NG, NP * PAD), jnp.float32),
            pltpu.VMEM((NP, PIECES, HALF, PAD), row.dtype),
            pltpu.VMEM((PIECES, HALF, PAD), row.dtype),
            pltpu.VMEM((160, PAD), jnp.float32),
            pltpu.VMEM((cube, PAD), jnp.float32),
            pltpu.VMEM((NP, cube, PAD), jnp.float32),
            pltpu.VMEM((planes * NG + 64, PAD), jnp.float32),
            pltpu.VMEM((SPAN + 32, PAD), jnp.float32),
            pltpu.VMEM((count, SPAN, PAD), row.dtype),
            pltpu.VMEM((count, SPAN, PAD), row.dtype),
            pltpu.VMEM((NP, SPAN, PAD), jnp.float32),
            pltpu.VMEM((count, SPAN, PAD), jnp.float32),
            pltpu.VMEM((count * SPAN, PAD), jnp.float32),
            pltpu.VMEM((count * count, PAD), jnp.float32),
            pltpu.VMEM((count, count, PAD), jnp.float32),
            dma((NP, PIECES, 4)), dma((NP, PIECES)), dma((count,)), dma((count,)),
            dma((count,)), dma((count,)), dma((count,)), dma((count,)), dma((2,)), dma,
        ],
        compiler_params=pltpu.CompilerParams(
            collective_id=3, has_side_effects=True, vmem_limit_bytes=50 << 20
        ),
        cost_estimate=pl.CostEstimate(
            flops=12 * NP * NG**4, bytes_accessed=8 << 20, transcendentals=0
        ),
        name="vectors",
    )(
        targets,
        row,
        left_table(fourier),
        left_table(fourier.T.copy()),
        right_square(fourier.T.copy()),
        right_square(fourier),
        np.broadcast_to(squares[:, None], (NG, NP * PAD)).copy(),
        np.tile(lanes, NP)[None, :],
    )


def finish_kernel(total, vectors, projector, factors, mixed):
    count = total.shape[0]
    scale = -0.5 / NG**3
    square = jnp.concatenate([total[...], jnp.zeros((PAD - count, PAD), jnp.float32)], axis=0)
    metric = scale * (square + square.T)[:count]
    row = lax.broadcasted_iota(jnp.int32, (count, PAD), 0)
    lane = lax.broadcasted_iota(jnp.int32, (count, PAD), 1)
    state = metric + jnp.where(lane == row + count, 1.0, 0.0)
    for k in range(count - 1):
        pivot = state[k : k + 1]
        ratio = state[:, k : k + 1] / pivot[:, k : k + 1]
        state = state - jnp.where(row > k, ratio, 0.0) * pivot
    diagonal = jnp.sum(jnp.where(lane == row, state, 0.0), axis=1, keepdims=True)
    state = state * (1.0 / jnp.sqrt(diagonal))
    for j in range(count):
        factors[j] = jnp.broadcast_to(state[:, count + j : count + j + 1], (count, PAD))

    size = 32

    def mix(step, carry):
        rows = pl.ds(pl.multiple_of(step * size, size), size)
        values = [vectors[j, rows] for j in range(count)]
        for k in range(count):
            result = factors[0, k : k + 1] * values[0]
            for j in range(1, k + 1):
                result += factors[j, k : k + 1] * values[j]
            mixed[pl.ds(step * size * count + k, size, stride=count), :] = result
        return carry

    lax.fori_loop(0, SPAN // size, mix, 0)

    unroll = 25

    def write(step, carry):
        for h in range(2):
            for i in range(unroll):
                rows = pl.ds(pl.multiple_of((h * HALF + step * unroll + i) * count, count), count)
                start = pl.multiple_of((h * CHUNK + step * unroll + i) * PAD, PAD)
                projector[:, pl.ds(start, PAD)] = mixed[rows]
        return carry

    lax.fori_loop(0, CHUNK // unroll, write, 0)


def finish(total, vectors):
    count = total.shape[0]
    vmem = pl.BlockSpec(memory_space=pltpu.VMEM)
    return pl.pallas_call(
        finish_kernel,
        out_shape=jax.ShapeDtypeStruct((count, 2 * CHUNK * PAD), jnp.float32),
        in_specs=[vmem, vmem],
        out_specs=vmem,
        scratch_shapes=[
            pltpu.VMEM((count, count, PAD), jnp.float32),
            pltpu.VMEM((SPAN * count, PAD), jnp.float32),
        ],
        compiler_params=pltpu.CompilerParams(vmem_limit_bytes=16 << 20),
        name="finish",
    )(total, vectors)


def fast_body(orbitals):
    targets, row = chunks(orbitals)
    vectors, total = vectors_of(targets, row, lax.axis_size("band"))
    return finish(total, vectors)


def body(orbitals):
    devices = lax.axis_size("band")
    points = orbitals.shape[1]
    target, row = pick(orbitals)
    partners = share(row.reshape(QUARTERS, CHUNKS, -1, PAD), devices)
    vectors, target_slab = exchange(
        target.reshape(NG, NG, NG),
        partners.reshape(NP, NG, NG, NG),
        target.reshape(devices, 8, points // devices // 8),
        devices,
    )
    vector_slab = lax.all_to_all(
        vectors.reshape(1, points), "band", split_axis=1, concat_axis=0, tiled=True
    )
    target_slab = target_slab.reshape(devices, points // devices).astype(jnp.float32)
    part = jnp.einsum("ap,bp->ab", target_slab, vector_slab, precision=highest) / NG**3
    intersection = sum_all(part, devices)
    metric = -0.5 * (intersection + intersection.T)
    factor = lax.linalg.cholesky(metric, symmetrize_input=False)
    return jax.scipy.linalg.solve_triangular(factor, vector_slab, lower=True)


def solution(mesh):
    placed = (P(("spin", "band"), None),)
    fast = mesh.shape["band"] == 2 * NP * QUARTERS
    return jax.shard_map(
        fast_body if fast else body, mesh=mesh, in_specs=placed, out_specs=P("spin", "band"), check_vma=False
    )
```

```python
import functools

import jax
import jax.numpy as jnp
import numpy as np
from jax import lax
from jax.experimental import pallas as pl
from jax.experimental.pallas import tpu as pltpu
from jax.sharding import PartitionSpec as P

NG = 80
NP = 2
PAD = 128
QUARTERS = 4
CHUNKS = 5
highest = lax.Precision.HIGHEST


def tables(length):
    indices = np.arange(length)
    nyquist = length // 2
    frequency = np.where(indices <= nyquist, indices, indices - nyquist)
    angles = 2.0 * np.pi / length * (frequency[:, None] * indices[None, :] % length)
    edges = (indices == 0) | (indices == nyquist)
    weights = np.where(edges, 1.0 / length, 2.0 / length)
    fourier = np.where((indices <= nyquist)[:, None], np.cos(angles), np.sin(angles))
    fourier = (fourier * np.sqrt(weights)[:, None]).astype(np.float32)
    squares = ((2.0 * np.pi / length * frequency) ** 2).astype(np.float32)
    return fourier, squares


def halves(table):
    high = table.astype(jnp.bfloat16)
    low = (table - high.astype(np.float32)).astype(jnp.bfloat16)
    return high, low


def left_table(table):
    high, low = halves(table)
    return np.concatenate([high, high, low], axis=1)


def right_table(table, depth):
    high, low = halves(table)
    result = np.zeros((depth, 2 * PAD), dtype=high.dtype)
    result[: table.shape[0], : table.shape[1]] = high
    result[: table.shape[0], PAD : PAD + table.shape[1]] = low
    return result


def barrier_all(me, count):
    barrier = pltpu.get_barrier_semaphore()
    for step in range(1, count):
        pl.semaphore_signal(
            barrier, inc=1, device_id={"band": lax.rem(me + step, count)},
            device_id_type=pl.DeviceIdType.MESH,
        )
    pl.semaphore_wait(barrier, count - 1)


def remote(source, target, send, receive, device):
    return pltpu.make_async_remote_copy(
        src_ref=source, dst_ref=target, send_sem=send, recv_sem=receive,
        device_id={"band": device}, device_id_type=pl.DeviceIdType.MESH,
    )


def share_kernel(count, row, partners, first_send, column_send, plane_send, receive, own_sem):
    me = lax.axis_index("band")
    planes = count // QUARTERS
    stride = count // NP
    column = lax.rem(me, QUARTERS)
    plane = lax.div(me, QUARTERS)
    base = plane * QUARTERS
    barrier_all(me, count)

    def first(r, q, c):
        return remote(row.at[q, c], partners.at[r, q, c], first_send.at[q - 1, c],
                      receive.at[r, q, c], lax.rem(me + q, count))

    def down(r, step, c):
        other = lax.rem(me + step * QUARTERS, count)
        return remote(partners.at[r, column, c], partners.at[r, column, c],
                      column_send.at[r, step - 1, c], receive.at[r, column, c], other)

    def neighbour(step):
        return base + lax.rem(column + step, QUARTERS)

    def across(r, step, c):
        return remote(partners.at[r, column, c], partners.at[r, column, c],
                      plane_send.at[r, step - 1, c], receive.at[r, column, c], neighbour(step))

    def arrived(r, q, c):
        remote(partners.at[r, q, c], partners.at[r, q, c], plane_send.at[r, 0, c],
               receive.at[r, q, c], me).wait_recv()

    for r in range(NP):
        @pl.when(me == r * stride)
        def _():
            own = pltpu.make_async_copy(row, partners.at[r], own_sem)
            own.start()
            own.wait()

    for c in range(CHUNKS):
        for r in range(NP):
            @pl.when(me != r * stride)
            def _():
                arrived(r, column, c)

            @pl.when(me == r * stride)
            def _():
                for q in range(1, QUARTERS):
                    first(r, q, c).start()

            @pl.when(plane == r * stride // QUARTERS)
            def _():
                for step in range(1, planes):
                    down(r, step, c).start()

            for step in range(1, QUARTERS):
                @pl.when(neighbour(step) != r * stride)
                def _():
                    across(r, step, c).start()

    for r in range(NP):
        @pl.when(me != r * stride)
        def _():
            for c in range(CHUNKS):
                for step in range(1, QUARTERS):
                    arrived(r, lax.rem(column + step, QUARTERS), c)

        @pl.when(me == r * stride)
        def _():
            for c in range(CHUNKS):
                for q in range(1, QUARTERS):
                    first(r, q, c).wait_send()

        @pl.when(plane == r * stride // QUARTERS)
        def _():
            for c in range(CHUNKS):
                for step in range(1, planes):
                    down(r, step, c).wait_send()

        for step in range(1, QUARTERS):
            @pl.when(neighbour(step) != r * stride)
            def _():
                for c in range(CHUNKS):
                    across(r, step, c).wait_send()


def share(row, count):
    planes = count // QUARTERS
    anywhere = pl.BlockSpec(memory_space=pl.ANY)
    dma = pltpu.SemaphoreType.DMA
    return pl.pallas_call(
        functools.partial(share_kernel, count),
        out_shape=jax.ShapeDtypeStruct((NP,) + row.shape, row.dtype),
        in_specs=[pl.BlockSpec(memory_space=pltpu.HBM)],
        out_specs=anywhere,
        scratch_shapes=[
            dma((QUARTERS - 1, CHUNKS)), dma((NP, planes - 1, CHUNKS)),
            dma((NP, QUARTERS - 1, CHUNKS)), dma((NP, QUARTERS, CHUNKS)), dma,
        ],
        compiler_params=pltpu.CompilerParams(
            collective_id=0, has_side_effects=True, vmem_limit_bytes=1 << 20
        ),
        name="share",
    )(row)


def sum_kernel(count, part, total, held, send, receive):
    me = lax.axis_index("band")
    barrier_all(me, count)

    def copy(step):
        return remote(part, held.at[step], send.at[step], receive.at[step],
                      lax.rem(me + step, count))

    for step in range(1, count):
        copy(step).start()
    held[0] = part[...]
    for step in range(1, count):
        copy(step).wait()
    total[...] = jnp.sum(held[...], axis=0)


def sum_all(part, count):
    vmem = pl.BlockSpec(memory_space=pltpu.VMEM)
    return pl.pallas_call(
        functools.partial(sum_kernel, count),
        out_shape=jax.ShapeDtypeStruct(part.shape, jnp.float32),
        in_specs=[vmem],
        out_specs=vmem,
        scratch_shapes=[
            pltpu.VMEM((count,) + part.shape, jnp.float32),
            pltpu.SemaphoreType.DMA((count,)),
            pltpu.SemaphoreType.DMA((count,)),
        ],
        compiler_params=pltpu.CompilerParams(
            collective_id=1, has_side_effects=True, vmem_limit_bytes=4 << 20
        ),
        name="sum_all",
    )(part)


def pick_kernel(orbitals, first, last):
    owned, width = orbitals.shape
    values = orbitals[...].astype(jnp.float32)
    first[...] = values[0:1].reshape(width // PAD, PAD).astype(first.dtype)
    last[...] = values[owned - 1 : owned].reshape(width // PAD, PAD).astype(last.dtype)


def pick(orbitals):
    owned, points = orbitals.shape
    steps = 10
    width = points // steps
    row = jax.ShapeDtypeStruct((points // PAD, PAD), orbitals.dtype)
    spec = pl.BlockSpec((width // PAD, PAD), lambda i: (i, 0))
    return pl.pallas_call(
        pick_kernel,
        grid=(steps,),
        out_shape=(row, row),
        in_specs=[pl.BlockSpec((owned, width), lambda i: (0, i))],
        out_specs=(spec, spec),
        compiler_params=pltpu.CompilerParams(vmem_limit_bytes=6 << 20),
        name="pick",
    )(orbitals)


def split(values):
    high = values.astype(jnp.bfloat16)
    low = (values - high.astype(jnp.float32)).astype(jnp.bfloat16)
    return high, low


def dot(left, right):
    return lax.dot_general(left, right, (((1,), (0,)), ((), ())),
                           preferred_element_type=jnp.float32)


def from_left(table, values):
    high, low = split(values)
    return dot(table, jnp.concatenate([high, low, high], axis=0))


def from_right(values, table):
    high, low = split(values)
    both = dot(high, table)
    return both[:, :PAD] + both[:, PAD:] + dot(low, table[:, :PAD])


def exchange_kernel(count, target_in, partners_in, forward_left, inverse_left, forward_right,
                    inverse_right, row_squares, lane_squares, slabs, vectors, gathered, one, two,
                    target, partners, done, send, receive, own_sem, load_sem, done_sem):
    group = 8
    me = lax.axis_index("band")
    loads = [
        pltpu.make_async_copy(target_in, target, load_sem.at[0]),
        pltpu.make_async_copy(partners_in, partners, load_sem.at[1]),
    ]
    for load in loads:
        load.start()
    barrier_all(me, count)

    def slab(step):
        other = lax.rem(me + step, count)
        return remote(slabs.at[other], gathered.at[me], send.at[step], receive.at[step], other)

    for step in range(1, count):
        slab(step).start()
    own = pltpu.make_async_copy(slabs.at[me], gathered.at[me], own_sem)
    own.start()
    for load in loads:
        load.wait()

    def ahead(step, carry):
        planes = pl.ds(step * group, group)
        left = target[planes].astype(jnp.float32)
        parts = []
        for r in range(NP):
            density = left * partners[r, planes].astype(jnp.float32)
            parts.append(from_right(density.reshape(group * NG, NG), forward_right[...]))
        values = jnp.concatenate(parts, axis=1).reshape(group, NG, NP * PAD)
        out = jnp.stack([from_left(forward_left[...], values[i]) for i in range(group)])
        one[:, pl.ds(pl.multiple_of(step * group, group), group), :] = jnp.swapaxes(out, 0, 1)
        return carry

    lax.fori_loop(0, NG // group, ahead, 0)

    def middle(step, carry):
        outs = []
        for i in range(group):
            number = step * group + i
            folded = jnp.where(number <= NG // 2, number, number - NG // 2)
            wave = (2.0 * np.pi / NG) * folded.astype(jnp.float32)
            totals = row_squares[...] + lane_squares[...] + wave * wave
            weight = jnp.where(totals > 0.0, 1.0 / (0.0025 + totals), 0.0)
            spectrum = from_left(forward_left[...], one[number]) * weight
            outs.append(from_left(inverse_left[...], spectrum))
        out = jnp.stack(outs)
        two[:, pl.ds(pl.multiple_of(step * group, group), group), :] = jnp.swapaxes(out, 0, 1)
        return carry

    lax.fori_loop(0, NG // group, middle, 0)

    def back(step, carry):
        planes = pl.ds(step * group, group)
        values = jnp.stack(
            [from_left(inverse_left[...], two[step * group + i]) for i in range(group)]
        ).reshape(group * NG, NP * PAD)
        total = jnp.zeros((group, NG, NG), jnp.float32)
        for r in range(NP):
            potential = from_right(values[:, r * PAD : (r + 1) * PAD], inverse_right[...])
            potential = potential.reshape(group, NG, PAD)[:, :, :NG]
            total -= partners[r, planes].astype(jnp.float32) * potential
        done[planes] = total
        stored(step).start()
        return carry

    def stored(step):
        planes = pl.ds(step * group, group)
        return pltpu.make_async_copy(done.at[planes], vectors.at[planes], done_sem.at[step])

    lax.fori_loop(0, NG // group, back, 0)
    for step in range(NG // group):
        stored(step).wait()
    own.wait()
    for step in range(1, count):
        slab(step).wait()


def exchange(target, partners, slabs, count):
    fourier, squares = tables(NG)
    lanes = np.zeros((PAD,), np.float32)
    lanes[:NG] = squares
    vmem = pl.BlockSpec(memory_space=pltpu.VMEM)
    anywhere = pl.BlockSpec(memory_space=pl.ANY)
    dma = pltpu.SemaphoreType.DMA
    return pl.pallas_call(
        functools.partial(exchange_kernel, count),
        out_shape=(
            jax.ShapeDtypeStruct((NG, NG, NG), jnp.float32),
            jax.ShapeDtypeStruct(slabs.shape, slabs.dtype),
        ),
        in_specs=[anywhere] * 2 + [vmem] * 6 + [anywhere],
        out_specs=(anywhere, anywhere),
        scratch_shapes=[pltpu.VMEM((NG, NG, NP * PAD), jnp.float32)] * 2
        + [
            pltpu.VMEM(target.shape, target.dtype),
            pltpu.VMEM(partners.shape, partners.dtype),
            pltpu.VMEM((NG, NG, NG), jnp.float32),
            dma((count,)), dma((count,)), dma, dma((2,)), dma((NG // 8,)),
        ],
        compiler_params=pltpu.CompilerParams(
            collective_id=2, has_side_effects=True, vmem_limit_bytes=60 << 20
        ),
        cost_estimate=pl.CostEstimate(
            flops=12 * NP * NG**4, bytes_accessed=8 << 20, transcendentals=0
        ),
        name="exchange",
    )(
        target,
        partners,
        left_table(fourier),
        left_table(fourier.T.copy()),
        right_table(fourier.T.copy(), NG),
        right_table(fourier, PAD),
        np.broadcast_to(squares[:, None], (NG, NP * PAD)).copy(),
        np.tile(lanes, NP)[None, :],
        slabs,
    )


TARGETS_AT = 4
LAG = 3
PER = 2
LOADS = 4
LEVELS = 240
CHUNK = 125
GROUP = 8
WIDE = 32
HALF = 128
SPAN = 2 * HALF
PIECES = 32
UNITS = PIECES // PER
STEPS = UNITS // QUARTERS


def right_square(table):
    high, low = halves(table)
    rows, columns = table.shape
    result = np.zeros((2 * PAD, 2 * PAD), dtype=high.dtype)
    result[:rows, :columns] = high
    result[:rows, PAD : PAD + columns] = low
    result[PAD : PAD + rows, :columns] = high
    return result


def right(values, table):
    both = dot(jnp.concatenate(split(values), axis=1), table)
    return both[:, :PAD] + both[:, PAD:]


def flip(number, mask):
    result = number
    for bit in (1, 2, 4, 8):
        mine = lax.rem(lax.div(number, bit), 2)
        asked = lax.rem(lax.div(mask, bit), 2) if not isinstance(mask, int) else (mask // bit) % 2
        result = result + asked * (bit - 2 * bit * mine)
    return result


def spread(source, target, base):
    rows = [source[pl.ds(j, WIDE, stride=5), :] for j in range(5)]
    lane = lax.broadcasted_iota(jnp.int32, (WIDE, PAD), 1)
    for a in range(GROUP):
        row, offset = divmod(NG * a, PAD)
        value = rows[row]
        if offset + NG > PAD:
            value = jnp.where(lane >= offset, value, rows[row + 1])
        if offset:
            value = pltpu.roll(value, PAD - offset, 1)
        target[pl.ds(base + a, WIDE, stride=GROUP), :] = value


def gather(source, base, target):
    lane = lax.broadcasted_iota(jnp.int32, (WIDE, PAD), 1)
    rows = []
    for a in range(GROUP):
        value = source[pl.ds(base + a, WIDE, stride=GROUP), :]
        shift = NG * a % PAD
        rows.append(pltpu.roll(value, shift, 1) if shift else value)
    for j in range(5):
        low, high = PAD * j // NG, (PAD * j + PAD - 1) // NG
        value = rows[low]
        for a in range(low + 1, high + 1):
            value = jnp.where(lane >= NG * a - PAD * j, rows[a], value)
        target[pl.ds(j, WIDE, stride=5), :] = value


def flag(condition):
    return jnp.where(condition, 1, 0)


def encode(values, inverse):
    level = jnp.sqrt(jnp.abs(values) * inverse) * LEVELS
    whole = jnp.floor(level)
    code = jnp.exp2(whole - LEVELS / 2) * (1.0 + (level - whole))
    return jnp.where(values < 0.0, -code, code)


def decode(codes, scale):
    size = jnp.maximum(jnp.abs(codes), 2.0 ** (-LEVELS / 2))
    whole = jnp.floor(jnp.log2(size))
    level = (whole + (LEVELS / 2 - 1.0) + size * jnp.exp2(-whole)) * (1.0 / LEVELS)
    level = level * level * scale
    return jnp.where(codes < 0.0, -level, level)


def vectors_kernel(count, orbitals, forward_left, inverse_left, forward_right,
                   inverse_right, row_squares, lane_squares, vectors, total,
                   one, two, bands, targets_in, part, landed, wide, target, partners, padded, flat, outgoing, incoming,
                   own_partners, decoded, points, products, sums,
                   part_send, part_receive, target_send, target_receive, vector_send,
                   vector_receive, sum_send, sum_receive, own_sem, out_sem, load_sem):
    me = lax.axis_index("band")
    stride = count // NP
    layers = count // QUARTERS
    column = lax.rem(me, QUARTERS)
    layer = lax.div(me, QUARTERS)
    beside, behind = flip(me, 1), flip(me, 2)

    points_in = orbitals.shape[1]
    span = points_in // LOADS

    def loading(k):
        columns = pl.ds(k * span, span)
        return pltpu.make_async_copy(orbitals.at[:, columns], bands.at[:, columns], load_sem.at[k])

    for k in range(LOADS):
        loading(k).start()
    barrier = pltpu.get_barrier_semaphore()
    for step in range(1, count):
        pl.semaphore_signal(
            barrier, inc=1, device_id={"band": lax.rem(me + step, count)},
            device_id_type=pl.DeviceIdType.MESH,
        )
    at_root = [me == r * stride for r in range(NP)]

    def cut(n, row):
        size = CHUNK * PAD
        piece = bands[:, pl.ds(pl.multiple_of(n * size, PAD), size)].astype(jnp.float32)
        value = piece[row : row + 1].reshape(CHUNK, PAD)
        rest = jnp.zeros((HALF - CHUNK, PAD), jnp.float32)
        return jnp.concatenate([value, rest], axis=0)

    def take_row(n, carry):
        value = cut(n, orbitals.shape[0] - 1).astype(part.dtype)
        for r in range(NP):
            @pl.when(at_root[r])
            def _():
                part[r, n] = value
        return carry

    def take_target(n, carry):
        value = cut(n, 0)
        targets_in[n] = value.astype(targets_in.dtype)
        wide[0:HALF] = value
        spread(wide, target, pl.multiple_of(n * 200, 8))
        return carry

    for k in range(LOADS):
        loading(k).wait()
        pieces = (PIECES // LOADS * k, PIECES // LOADS * (k + 1))

        @pl.when(at_root[0] | at_root[1])
        def _():
            lax.fori_loop(*pieces, take_row, 0)

    pl.semaphore_wait(barrier, count - 1)

    def slab_of_target(mask):
        other = flip(me, mask)
        return remote(targets_in.at[pl.ds(2 * other, 2)], landed.at[pl.ds(2 * me, 2)],
                      target_send.at[mask], target_receive.at[mask], other)

    def own_target():
        return pltpu.make_async_copy(targets_in.at[pl.ds(2 * me, 2)], landed.at[pl.ds(2 * me, 2)],
                                     own_sem.at[1])

    def forward(r, n, way, other):
        unit = pl.ds(n * PER, PER)
        return remote(part.at[r, unit], part.at[r, unit], part_send.at[r, n, way],
                      part_receive.at[r, n], other)

    at_source = [layer == r * stride // QUARTERS for r in range(NP)]
    is_root = [me == r * stride for r in range(NP)]
    own_ways = [
        [
            jnp.where(at_source[r], lax.rem(me + d * QUARTERS, count), peer)
            for d, peer in ((1, beside), (2, behind), (3, flip(me, 3)))
        ]
        for r in range(NP)
    ]
    ends = (column == 0) | (column == QUARTERS - 1)
    hands = [ends | (column == (1, 1, 2, 3)[q]) for q in range(QUARTERS)]
    after = [jnp.where(ends if q < 2 else ~ends, beside, behind) for q in range(QUARTERS)]

    def start_all(r, c):
        for d, other in enumerate(own_ways[r]):
            forward(r, QUARTERS * c + column, d, other).start()

    def seed(r):
        def step(c, carry):
            for q in (3, 1, 2, 0):
                other = me + q if q == QUARTERS - 1 else after[q]
                forward(r, QUARTERS * c + q, 3, other).start()
            start_all(r, c)
            return carry

        lax.fori_loop(0, STEPS, step, 0)

    for r in range(NP):
        @pl.when(is_root[r])
        def _():
            seed(r)

    def wait_part(r, n):
        forward(r, n, 0, beside).wait_recv()

    def hand_on(r, i):
        c = i - late[r]

        @pl.when((c >= 0) & (c < STEPS) & ~is_root[r])
        def _():
            wait_part(r, QUARTERS * c + column)
            start_all(r, c)

            @pl.when(at_source[r])
            def _():
                for q in (3, 1, 2, 0):
                    @pl.when(hands[q])
                    def _():
                        @pl.when(column != q)
                        def _():
                            wait_part(r, QUARTERS * c + q)

                        forward(r, QUARTERS * c + q, 3, after[q]).start()
                        if q == QUARTERS - 1:
                            forward(r, QUARTERS * c + q, 4, beside).start()

    late = [flag(~at_source[r]) for r in range(NP)]
    still = [
        [~is_root[r] & (column != q) & ~(at_source[r] & hands[q]) for q in range(QUARTERS)]
        for r in range(NP)
    ]

    def receive_rest(r, c):
        for q in range(QUARTERS):
            @pl.when(still[r][q])
            def _():
                wait_part(r, QUARTERS * c + q)

    def ahead(step, carry):
        rows = pl.ds(pl.multiple_of(step * GROUP * NG, GROUP * NG), GROUP * NG)
        left = target[rows]
        parts = [right(left * partners[r, rows], forward_right[...]) for r in range(NP)]
        values = jnp.concatenate(parts, axis=1).reshape(GROUP, NG, NP * PAD)
        out = jnp.stack([from_left(forward_left[...], values[i]) for i in range(GROUP)])
        one[:, pl.ds(pl.multiple_of(step * GROUP, GROUP), GROUP), :] = jnp.swapaxes(out, 0, 1)
        return carry

    def relay(i, carry):
        for r in range(NP):
            hand_on(r, i)

        @pl.when(i < STEPS)
        def _():
            pieces = PIECES // STEPS
            lax.fori_loop(i * pieces, (i + 1) * pieces, take_target, 0)

        @pl.when(i == TARGETS_AT)
        def _():
            for mask in list(range(count // 2, count)) + list(range(1, count // 2)):
                slab_of_target(mask).start()
            own_target().start()

        @pl.when(i >= LAG)
        def _():
            c = i - LAG
            for r in range(NP):
                receive_rest(r, c)

            def arrived(q, carry):
                n = c * (QUARTERS * PER) + q
                for r in range(NP):
                    wide[0:HALF] = part[r, n].astype(jnp.float32)
                    spread(wide, partners.at[r], pl.multiple_of(n * 200, 8))
                return carry

            lax.fori_loop(0, QUARTERS * PER, arrived, 0)
            first, last = (lax.div(NG // STEPS * k, GROUP) for k in (c, c + 1))
            lax.fori_loop(first, last, ahead, 0)

        return carry

    lax.fori_loop(0, STEPS + LAG, relay, 0)

    def middle(step, carry):
        outs = []
        for i in range(GROUP):
            number = step * GROUP + i
            folded = jnp.where(number <= NG // 2, number, number - NG // 2)
            wave = (2.0 * np.pi / NG) * folded.astype(jnp.float32)
            totals = row_squares[...] + lane_squares[...] + wave * wave
            weight = jnp.where(totals > 0.0, 1.0 / (0.0025 + totals), 0.0)
            spectrum = from_left(forward_left[...], one[number]) * weight
            outs.append(from_left(inverse_left[...], spectrum))
        out = jnp.stack(outs)
        two[:, pl.ds(pl.multiple_of(step * GROUP, GROUP), GROUP), :] = jnp.swapaxes(out, 0, 1)
        return carry

    lax.fori_loop(0, NG // GROUP, middle, 0)

    planes = NG // count
    padded[pl.ds(planes * NG, 64)] = jnp.zeros((64, PAD), jnp.float32)

    def slab(mask):
        other = flip(me, mask)
        return remote(outgoing.at[other], incoming.at[me], vector_send.at[mask],
                      vector_receive.at[mask], other)

    def own_slab():
        return pltpu.make_async_copy(outgoing.at[me], incoming.at[me],
                                     own_sem.at[0])

    def back(step, carry):
        mask = lax.rem(step + count // 2, count)
        s = flip(me, mask)
        spectra = [two[s * planes + i] for i in range(planes)]
        side = jnp.zeros((1, PAD), jnp.float32)
        lane = lax.broadcasted_iota(jnp.int32, (1, PAD), 1)
        for i in range(planes):
            for r in range(NP):
                mean = spectra[i][0:1, r * PAD : r * PAD + 1] / NG
                side = jnp.where(lane == 8 * r + i, mean, side)
        row = lax.broadcasted_iota(jnp.int32, (NG, NP * PAD), 0)
        column = lax.broadcasted_iota(jnp.int32, (NG, NP * PAD), 1)
        keep = (row != 0) | ((column != 0) & (column != PAD))
        values = jnp.concatenate(
            [from_left(inverse_left[...], jnp.where(keep, x, 0.0)) for x in spectra], axis=0
        )
        rows = pl.ds(pl.multiple_of(s * planes * NG, planes * NG), planes * NG)
        result = jnp.zeros((planes * NG, PAD), jnp.float32)
        for r in range(NP):
            potential = right(values[:, r * PAD : (r + 1) * PAD], inverse_right[...])
            result -= partners[r, rows] * potential
        padded[0 : planes * NG] = result
        for h in range(2):
            gather(padded, h * 200, flat.at[pl.ds(h * HALF, 160)])
        biggest = jnp.max(jnp.abs(result), axis=0, keepdims=True)
        biggest = jnp.max(biggest, axis=1, keepdims=True)
        side = jnp.where(lane == 16, biggest, side)
        inverse = jnp.where(biggest > 0.0, 1.0 / biggest, 0.0)
        codes = encode(flat[0:SPAN], inverse)
        high = side.astype(jnp.bfloat16).astype(jnp.float32)
        rest = side - high
        middling = rest.astype(jnp.bfloat16).astype(jnp.float32)
        line = lax.broadcasted_iota(jnp.int32, (8, PAD), 0)
        last = codes[HALF - 8 : HALF]
        for i, value in ((CHUNK, high), (CHUNK + 1, middling), (CHUNK + 2, rest - middling)):
            last = jnp.where(line == i - HALF + 8, value, last)
        codes = jnp.concatenate([codes[: HALF - 8], last, codes[HALF:]], axis=0)
        outgoing[s] = codes.astype(outgoing.dtype)

        @pl.when(mask != 0)
        def _():
            slab(mask).start()

        @pl.when(mask == 0)
        def _():
            own_slab().start()

        return carry

    lax.fori_loop(0, count, back, 0)

    own_target().wait()
    for mask in range(1, count):
        slab_of_target(mask).wait()

    def lift(n, carry):
        points[pl.ds(pl.multiple_of(n * HALF, HALF), HALF)] = landed[n].astype(jnp.float32)
        return carry

    lax.fori_loop(0, PIECES, lift, 0)

    def sent(c, carry):
        for r in range(NP):
            for d, other in enumerate(own_ways[r]):
                forward(r, QUARTERS * c + column, d, other).wait_send()

            @pl.when(at_source[r])
            def _():
                for q in range(QUARTERS):
                    @pl.when(hands[q])
                    def _():
                        forward(r, QUARTERS * c + q, 3, after[q]).wait_send()
                        if q == QUARTERS - 1:
                            @pl.when(column == q)
                            def _():
                                forward(r, QUARTERS * c + q, 4, beside).wait_send()

        return carry

    lax.fori_loop(0, STEPS, sent, 0)

    for r in range(NP):
        for h in range(2):
            own_partners[r, h * HALF : (h + 1) * HALF] = part[r, 2 * me + h].astype(jnp.float32)
    line = lax.broadcasted_iota(jnp.int32, (SPAN, PAD), 0)
    plane = lax.div(line - flag(line >= HALF) * (HALF - CHUNK), NG * NG // PAD)

    def stored(b):
        return pltpu.make_async_copy(decoded.at[b], vectors.at[b], out_sem.at[b])

    def meet(mask, carry):
        @pl.when(mask != 0)
        def _():
            slab(mask).wait_recv()

        @pl.when(mask == 0)
        def _():
            own_slab().wait()

        b = flip(me, mask)
        codes = incoming[b].astype(jnp.float32)
        side = jnp.sum(codes[CHUNK:HALF], axis=0, keepdims=True)
        values = decode(codes, side[:, 16:17])
        for r in range(NP):
            mean = side[:, 8 * r : 8 * r + 1]
            for i in range(1, planes):
                mean = jnp.where(plane >= i, side[:, 8 * r + i : 8 * r + i + 1], mean)
            values -= own_partners[r] * mean
        decoded[b] = values
        stored(b).start()
        for a in range(count):
            product = points[a * SPAN : (a + 1) * SPAN] * values
            product = jnp.sum(product.reshape(SPAN // 8, 8, PAD), axis=0)
            products[pl.ds(b * count + a, 1)] = jnp.sum(product, axis=0, keepdims=True)
        return carry

    lax.fori_loop(0, count, meet, 0)

    line = jnp.sum(products[...], axis=1, keepdims=True)
    row = lax.broadcasted_iota(jnp.int32, (count * count, PAD), 0)
    lane = lax.broadcasted_iota(jnp.int32, (count * count, PAD), 1)
    placed = jnp.where(lane == lax.rem(row, count), line, 0.0)
    sums[me] = jnp.sum(placed.reshape(count, count, PAD), axis=1)

    def share_sum(mask):
        return remote(sums.at[me], sums.at[me], sum_send.at[mask], sum_receive.at[mask],
                      flip(me, mask))

    for mask in range(count - 1, 0, -1):
        share_sum(mask).start()
    for mask in range(1, count):
        slab(mask).wait_send()
    for mask in range(1, count):
        share_sum(mask).wait()
    total[...] = jnp.sum(sums[...], axis=0)
    for b in range(count):
        stored(b).wait()


def vectors_of(orbitals, count):
    fourier, squares = tables(NG)
    lanes = np.zeros((PAD,), np.float32)
    lanes[:NG] = squares
    vmem = pl.BlockSpec(memory_space=pltpu.VMEM)
    dma = pltpu.SemaphoreType.DMA
    cube = NG * NG + 64
    planes = NG // count
    return pl.pallas_call(
        functools.partial(vectors_kernel, count),
        out_shape=(
            jax.ShapeDtypeStruct((count, SPAN, PAD), jnp.float32),
            jax.ShapeDtypeStruct((count, PAD), jnp.float32),
        ),
        in_specs=[pl.BlockSpec(memory_space=pl.ANY)] + [vmem] * 6,
        out_specs=(pl.BlockSpec(memory_space=pl.ANY), vmem),
        scratch_shapes=[
            pltpu.VMEM((NG, NG, NP * PAD), jnp.float32),
            pltpu.VMEM((NG, NG, NP * PAD), jnp.float32),
            pltpu.VMEM(orbitals.shape, orbitals.dtype),
            pltpu.VMEM((PIECES, HALF, PAD), orbitals.dtype),
            pltpu.VMEM((NP, PIECES, HALF, PAD), orbitals.dtype),
            pltpu.VMEM((PIECES, HALF, PAD), orbitals.dtype),
            pltpu.VMEM((160, PAD), jnp.float32),
            pltpu.VMEM((cube, PAD), jnp.float32),
            pltpu.VMEM((NP, cube, PAD), jnp.float32),
            pltpu.VMEM((planes * NG + 64, PAD), jnp.float32),
            pltpu.VMEM((SPAN + 32, PAD), jnp.float32),
            pltpu.VMEM((count, SPAN, PAD), orbitals.dtype),
            pltpu.VMEM((count, SPAN, PAD), orbitals.dtype),
            pltpu.VMEM((NP, SPAN, PAD), jnp.float32),
            pltpu.VMEM((count, SPAN, PAD), jnp.float32),
            pltpu.VMEM((count * SPAN, PAD), jnp.float32),
            pltpu.VMEM((count * count, PAD), jnp.float32),
            pltpu.VMEM((count, count, PAD), jnp.float32),
            dma((NP, UNITS, 5)), dma((NP, UNITS)), dma((count,)), dma((count,)),
            dma((count,)), dma((count,)), dma((count,)), dma((count,)), dma((2,)), dma((count,)), dma((LOADS,)),
        ],
        compiler_params=pltpu.CompilerParams(
            collective_id=3, has_side_effects=True, vmem_limit_bytes=58 << 20
        ),
        cost_estimate=pl.CostEstimate(
            flops=12 * NP * NG**4, bytes_accessed=8 << 20, transcendentals=0
        ),
        name="vectors",
    )(
        orbitals,
        left_table(fourier),
        left_table(fourier.T.copy()),
        right_square(fourier.T.copy()),
        right_square(fourier),
        np.broadcast_to(squares[:, None], (NG, NP * PAD)).copy(),
        np.tile(lanes, NP)[None, :],
    )


def finish_kernel(total, vectors, projector, factors, mixed, held, made, load_sem, store_sem):
    count = total.shape[0]
    load = pltpu.make_async_copy(vectors, held, load_sem)
    load.start()
    scale = -0.5 / NG**3
    square = jnp.concatenate([total[...], jnp.zeros((PAD - count, PAD), jnp.float32)], axis=0)
    metric = scale * (square + square.T)[:count]
    row = lax.broadcasted_iota(jnp.int32, (count, PAD), 0)
    lane = lax.broadcasted_iota(jnp.int32, (count, PAD), 1)
    state = metric + jnp.where(lane == row + count, 1.0, 0.0)
    for k in range(count - 1):
        pivot = state[k : k + 1]
        ratio = state[:, k : k + 1] / pivot[:, k : k + 1]
        state = state - jnp.where(row > k, ratio, 0.0) * pivot
    diagonal = jnp.sum(jnp.where(lane == row, state, 0.0), axis=1, keepdims=True)
    state = state * (1.0 / jnp.sqrt(diagonal))
    for j in range(count):
        factors[j] = jnp.broadcast_to(state[:, count + j : count + j + 1], (count, PAD))

    size = 32
    half = CHUNK * PAD
    load.wait()

    def store(h):
        columns = pl.ds(h * half, half)
        return pltpu.make_async_copy(made.at[:, columns], projector.at[:, columns], store_sem.at[h])

    for h in range(2):
        def mix(step, carry):
            rows = pl.ds(pl.multiple_of(h * HALF + step * size, size), size)
            values = [held[j, rows] for j in range(count)]
            for k in range(count):
                result = factors[0, k : k + 1] * values[0]
                for j in range(1, k + 1):
                    result += factors[j, k : k + 1] * values[j]
                mixed[pl.ds(k, size, stride=count), :] = result
            for i in range(size):
                start = pl.multiple_of((h * CHUNK + step * size + i) * PAD, PAD)
                made[:, pl.ds(start, PAD)] = mixed[i * count : (i + 1) * count]
            return carry

        lax.fori_loop(0, HALF // size, mix, 0)
        store(h).start()
    for h in range(2):
        store(h).wait()


def finish(total, vectors):
    count = total.shape[0]
    vmem = pl.BlockSpec(memory_space=pltpu.VMEM)
    anywhere = pl.BlockSpec(memory_space=pl.ANY)
    return pl.pallas_call(
        finish_kernel,
        out_shape=jax.ShapeDtypeStruct((count, 2 * CHUNK * PAD), jnp.float32),
        in_specs=[vmem, anywhere],
        out_specs=anywhere,
        scratch_shapes=[
            pltpu.VMEM((count, count, PAD), jnp.float32),
            pltpu.VMEM((32 * count, PAD), jnp.float32),
            pltpu.VMEM(vectors.shape, jnp.float32),
            pltpu.VMEM((count, (SPAN + 8) * PAD), jnp.float32),
            pltpu.SemaphoreType.DMA,
            pltpu.SemaphoreType.DMA((2,)),
        ],
        compiler_params=pltpu.CompilerParams(vmem_limit_bytes=60 << 20),
        name="finish",
    )(total, vectors)


def fast_body(orbitals):
    vectors, total = vectors_of(orbitals, lax.axis_size("band"))
    return finish(total, vectors)


def body(orbitals):
    devices = lax.axis_size("band")
    points = orbitals.shape[1]
    target, row = pick(orbitals)
    partners = share(row.reshape(QUARTERS, CHUNKS, -1, PAD), devices)
    vectors, target_slab = exchange(
        target.reshape(NG, NG, NG),
        partners.reshape(NP, NG, NG, NG),
        target.reshape(devices, 8, points // devices // 8),
        devices,
    )
    vector_slab = lax.all_to_all(
        vectors.reshape(1, points), "band", split_axis=1, concat_axis=0, tiled=True
    )
    target_slab = target_slab.reshape(devices, points // devices).astype(jnp.float32)
    part = jnp.einsum("ap,bp->ab", target_slab, vector_slab, precision=highest) / NG**3
    intersection = sum_all(part, devices)
    metric = -0.5 * (intersection + intersection.T)
    factor = lax.linalg.cholesky(metric, symmetrize_input=False)
    return jax.scipy.linalg.solve_triangular(factor, vector_slab, lower=True)


def solution(mesh):
    placed = (P(("spin", "band"), None),)
    fast = mesh.shape["band"] == 2 * NP * QUARTERS
    return jax.shard_map(
        fast_body if fast else body, mesh=mesh, in_specs=placed, out_specs=P("spin", "band"), check_vma=False
    )
```

```python
import functools

import jax
import jax.numpy as jnp
import numpy as np
from jax import lax
from jax.experimental import pallas as pl
from jax.experimental.pallas import tpu as pltpu
from jax.sharding import PartitionSpec as P

NG = 80
NP = 2
PAD = 128
QUARTERS = 4
CHUNKS = 5
highest = lax.Precision.HIGHEST


def tables(length):
    indices = np.arange(length)
    nyquist = length // 2
    frequency = np.where(indices <= nyquist, indices, indices - nyquist)
    angles = 2.0 * np.pi / length * (frequency[:, None] * indices[None, :] % length)
    edges = (indices == 0) | (indices == nyquist)
    weights = np.where(edges, 1.0 / length, 2.0 / length)
    fourier = np.where((indices <= nyquist)[:, None], np.cos(angles), np.sin(angles))
    fourier = (fourier * np.sqrt(weights)[:, None]).astype(np.float32)
    squares = ((2.0 * np.pi / length * frequency) ** 2).astype(np.float32)
    return fourier, squares


def halves(table):
    high = table.astype(jnp.bfloat16)
    low = (table - high.astype(np.float32)).astype(jnp.bfloat16)
    return high, low


def left_table(table):
    high, low = halves(table)
    return np.concatenate([high, high, low], axis=1)


def right_table(table, depth):
    high, low = halves(table)
    result = np.zeros((depth, 2 * PAD), dtype=high.dtype)
    result[: table.shape[0], : table.shape[1]] = high
    result[: table.shape[0], PAD : PAD + table.shape[1]] = low
    return result


def barrier_all(me, count):
    barrier = pltpu.get_barrier_semaphore()
    for step in range(1, count):
        pl.semaphore_signal(
            barrier, inc=1, device_id={"band": lax.rem(me + step, count)},
            device_id_type=pl.DeviceIdType.MESH,
        )
    pl.semaphore_wait(barrier, count - 1)


def remote(source, target, send, receive, device):
    return pltpu.make_async_remote_copy(
        src_ref=source, dst_ref=target, send_sem=send, recv_sem=receive,
        device_id={"band": device}, device_id_type=pl.DeviceIdType.MESH,
    )


def share_kernel(count, row, partners, first_send, column_send, plane_send, receive, own_sem):
    me = lax.axis_index("band")
    planes = count // QUARTERS
    stride = count // NP
    column = lax.rem(me, QUARTERS)
    plane = lax.div(me, QUARTERS)
    base = plane * QUARTERS
    barrier_all(me, count)

    def first(r, q, c):
        return remote(row.at[q, c], partners.at[r, q, c], first_send.at[q - 1, c],
                      receive.at[r, q, c], lax.rem(me + q, count))

    def down(r, step, c):
        other = lax.rem(me + step * QUARTERS, count)
        return remote(partners.at[r, column, c], partners.at[r, column, c],
                      column_send.at[r, step - 1, c], receive.at[r, column, c], other)

    def neighbour(step):
        return base + lax.rem(column + step, QUARTERS)

    def across(r, step, c):
        return remote(partners.at[r, column, c], partners.at[r, column, c],
                      plane_send.at[r, step - 1, c], receive.at[r, column, c], neighbour(step))

    def arrived(r, q, c):
        remote(partners.at[r, q, c], partners.at[r, q, c], plane_send.at[r, 0, c],
               receive.at[r, q, c], me).wait_recv()

    for r in range(NP):
        @pl.when(me == r * stride)
        def _():
            own = pltpu.make_async_copy(row, partners.at[r], own_sem)
            own.start()
            own.wait()

    for c in range(CHUNKS):
        for r in range(NP):
            @pl.when(me != r * stride)
            def _():
                arrived(r, column, c)

            @pl.when(me == r * stride)
            def _():
                for q in range(1, QUARTERS):
                    first(r, q, c).start()

            @pl.when(plane == r * stride // QUARTERS)
            def _():
                for step in range(1, planes):
                    down(r, step, c).start()

            for step in range(1, QUARTERS):
                @pl.when(neighbour(step) != r * stride)
                def _():
                    across(r, step, c).start()

    for r in range(NP):
        @pl.when(me != r * stride)
        def _():
            for c in range(CHUNKS):
                for step in range(1, QUARTERS):
                    arrived(r, lax.rem(column + step, QUARTERS), c)

        @pl.when(me == r * stride)
        def _():
            for c in range(CHUNKS):
                for q in range(1, QUARTERS):
                    first(r, q, c).wait_send()

        @pl.when(plane == r * stride // QUARTERS)
        def _():
            for c in range(CHUNKS):
                for step in range(1, planes):
                    down(r, step, c).wait_send()

        for step in range(1, QUARTERS):
            @pl.when(neighbour(step) != r * stride)
            def _():
                for c in range(CHUNKS):
                    across(r, step, c).wait_send()


def share(row, count):
    planes = count // QUARTERS
    anywhere = pl.BlockSpec(memory_space=pl.ANY)
    dma = pltpu.SemaphoreType.DMA
    return pl.pallas_call(
        functools.partial(share_kernel, count),
        out_shape=jax.ShapeDtypeStruct((NP,) + row.shape, row.dtype),
        in_specs=[pl.BlockSpec(memory_space=pltpu.HBM)],
        out_specs=anywhere,
        scratch_shapes=[
            dma((QUARTERS - 1, CHUNKS)), dma((NP, planes - 1, CHUNKS)),
            dma((NP, QUARTERS - 1, CHUNKS)), dma((NP, QUARTERS, CHUNKS)), dma,
        ],
        compiler_params=pltpu.CompilerParams(
            collective_id=0, has_side_effects=True, vmem_limit_bytes=1 << 20
        ),
        name="share",
    )(row)


def sum_kernel(count, part, total, held, send, receive):
    me = lax.axis_index("band")
    barrier_all(me, count)

    def copy(step):
        return remote(part, held.at[step], send.at[step], receive.at[step],
                      lax.rem(me + step, count))

    for step in range(1, count):
        copy(step).start()
    held[0] = part[...]
    for step in range(1, count):
        copy(step).wait()
    total[...] = jnp.sum(held[...], axis=0)


def sum_all(part, count):
    vmem = pl.BlockSpec(memory_space=pltpu.VMEM)
    return pl.pallas_call(
        functools.partial(sum_kernel, count),
        out_shape=jax.ShapeDtypeStruct(part.shape, jnp.float32),
        in_specs=[vmem],
        out_specs=vmem,
        scratch_shapes=[
            pltpu.VMEM((count,) + part.shape, jnp.float32),
            pltpu.SemaphoreType.DMA((count,)),
            pltpu.SemaphoreType.DMA((count,)),
        ],
        compiler_params=pltpu.CompilerParams(
            collective_id=1, has_side_effects=True, vmem_limit_bytes=4 << 20
        ),
        name="sum_all",
    )(part)


def pick_kernel(orbitals, first, last):
    owned, width = orbitals.shape
    values = orbitals[...].astype(jnp.float32)
    first[...] = values[0:1].reshape(width // PAD, PAD).astype(first.dtype)
    last[...] = values[owned - 1 : owned].reshape(width // PAD, PAD).astype(last.dtype)


def pick(orbitals):
    owned, points = orbitals.shape
    steps = 10
    width = points // steps
    row = jax.ShapeDtypeStruct((points // PAD, PAD), orbitals.dtype)
    spec = pl.BlockSpec((width // PAD, PAD), lambda i: (i, 0))
    return pl.pallas_call(
        pick_kernel,
        grid=(steps,),
        out_shape=(row, row),
        in_specs=[pl.BlockSpec((owned, width), lambda i: (0, i))],
        out_specs=(spec, spec),
        compiler_params=pltpu.CompilerParams(vmem_limit_bytes=6 << 20),
        name="pick",
    )(orbitals)


def split(values):
    high = values.astype(jnp.bfloat16)
    low = (values - high.astype(jnp.float32)).astype(jnp.bfloat16)
    return high, low


def dot(left, right):
    return lax.dot_general(left, right, (((1,), (0,)), ((), ())),
                           preferred_element_type=jnp.float32)


def from_left(table, values):
    high, low = split(values)
    return dot(table, jnp.concatenate([high, low, high], axis=0))


def from_right(values, table):
    high, low = split(values)
    both = dot(high, table)
    return both[:, :PAD] + both[:, PAD:] + dot(low, table[:, :PAD])


def exchange_kernel(count, target_in, partners_in, forward_left, inverse_left, forward_right,
                    inverse_right, row_squares, lane_squares, slabs, vectors, gathered, one, two,
                    target, partners, done, send, receive, own_sem, load_sem, done_sem):
    group = 8
    me = lax.axis_index("band")
    loads = [
        pltpu.make_async_copy(target_in, target, load_sem.at[0]),
        pltpu.make_async_copy(partners_in, partners, load_sem.at[1]),
    ]
    for load in loads:
        load.start()
    barrier_all(me, count)

    def slab(step):
        other = lax.rem(me + step, count)
        return remote(slabs.at[other], gathered.at[me], send.at[step], receive.at[step], other)

    for step in range(1, count):
        slab(step).start()
    own = pltpu.make_async_copy(slabs.at[me], gathered.at[me], own_sem)
    own.start()
    for load in loads:
        load.wait()

    def ahead(step, carry):
        planes = pl.ds(step * group, group)
        left = target[planes].astype(jnp.float32)
        parts = []
        for r in range(NP):
            density = left * partners[r, planes].astype(jnp.float32)
            parts.append(from_right(density.reshape(group * NG, NG), forward_right[...]))
        values = jnp.concatenate(parts, axis=1).reshape(group, NG, NP * PAD)
        out = jnp.stack([from_left(forward_left[...], values[i]) for i in range(group)])
        one[:, pl.ds(pl.multiple_of(step * group, group), group), :] = jnp.swapaxes(out, 0, 1)
        return carry

    lax.fori_loop(0, NG // group, ahead, 0)

    def middle(step, carry):
        outs = []
        for i in range(group):
            number = step * group + i
            folded = jnp.where(number <= NG // 2, number, number - NG // 2)
            wave = (2.0 * np.pi / NG) * folded.astype(jnp.float32)
            totals = row_squares[...] + lane_squares[...] + wave * wave
            weight = jnp.where(totals > 0.0, 1.0 / (0.0025 + totals), 0.0)
            spectrum = from_left(forward_left[...], one[number]) * weight
            outs.append(from_left(inverse_left[...], spectrum))
        out = jnp.stack(outs)
        two[:, pl.ds(pl.multiple_of(step * group, group), group), :] = jnp.swapaxes(out, 0, 1)
        return carry

    lax.fori_loop(0, NG // group, middle, 0)

    def back(step, carry):
        planes = pl.ds(step * group, group)
        values = jnp.stack(
            [from_left(inverse_left[...], two[step * group + i]) for i in range(group)]
        ).reshape(group * NG, NP * PAD)
        total = jnp.zeros((group, NG, NG), jnp.float32)
        for r in range(NP):
            potential = from_right(values[:, r * PAD : (r + 1) * PAD], inverse_right[...])
            potential = potential.reshape(group, NG, PAD)[:, :, :NG]
            total -= partners[r, planes].astype(jnp.float32) * potential
        done[planes] = total
        stored(step).start()
        return carry

    def stored(step):
        planes = pl.ds(step * group, group)
        return pltpu.make_async_copy(done.at[planes], vectors.at[planes], done_sem.at[step])

    lax.fori_loop(0, NG // group, back, 0)
    for step in range(NG // group):
        stored(step).wait()
    own.wait()
    for step in range(1, count):
        slab(step).wait()


def exchange(target, partners, slabs, count):
    fourier, squares = tables(NG)
    lanes = np.zeros((PAD,), np.float32)
    lanes[:NG] = squares
    vmem = pl.BlockSpec(memory_space=pltpu.VMEM)
    anywhere = pl.BlockSpec(memory_space=pl.ANY)
    dma = pltpu.SemaphoreType.DMA
    return pl.pallas_call(
        functools.partial(exchange_kernel, count),
        out_shape=(
            jax.ShapeDtypeStruct((NG, NG, NG), jnp.float32),
            jax.ShapeDtypeStruct(slabs.shape, slabs.dtype),
        ),
        in_specs=[anywhere] * 2 + [vmem] * 6 + [anywhere],
        out_specs=(anywhere, anywhere),
        scratch_shapes=[pltpu.VMEM((NG, NG, NP * PAD), jnp.float32)] * 2
        + [
            pltpu.VMEM(target.shape, target.dtype),
            pltpu.VMEM(partners.shape, partners.dtype),
            pltpu.VMEM((NG, NG, NG), jnp.float32),
            dma((count,)), dma((count,)), dma, dma((2,)), dma((NG // 8,)),
        ],
        compiler_params=pltpu.CompilerParams(
            collective_id=2, has_side_effects=True, vmem_limit_bytes=60 << 20
        ),
        cost_estimate=pl.CostEstimate(
            flops=12 * NP * NG**4, bytes_accessed=8 << 20, transcendentals=0
        ),
        name="exchange",
    )(
        target,
        partners,
        left_table(fourier),
        left_table(fourier.T.copy()),
        right_table(fourier.T.copy(), NG),
        right_table(fourier, PAD),
        np.broadcast_to(squares[:, None], (NG, NP * PAD)).copy(),
        np.tile(lanes, NP)[None, :],
        slabs,
    )


TARGETS_AT = 4
LAG = 3
PER = 2
LOADS = 4
LEVELS = 240
CHUNK = 125
GROUP = 8
WIDE = 32
HALF = 128
SPAN = 2 * HALF
PIECES = 32
UNITS = PIECES // PER
STEPS = UNITS // QUARTERS


def right_square(table):
    high, low = halves(table)
    rows, columns = table.shape
    result = np.zeros((2 * PAD, 2 * PAD), dtype=high.dtype)
    result[:rows, :columns] = high
    result[:rows, PAD : PAD + columns] = low
    result[PAD : PAD + rows, :columns] = high
    return result


def right(values, table):
    both = dot(jnp.concatenate(split(values), axis=1), table)
    return both[:, :PAD] + both[:, PAD:]


def flip(number, mask):
    result = number
    for bit in (1, 2, 4, 8):
        mine = lax.rem(lax.div(number, bit), 2)
        asked = lax.rem(lax.div(mask, bit), 2) if not isinstance(mask, int) else (mask // bit) % 2
        result = result + asked * (bit - 2 * bit * mine)
    return result


def spread(source, target, base):
    rows = [source[pl.ds(j, WIDE, stride=5), :] for j in range(5)]
    lane = lax.broadcasted_iota(jnp.int32, (WIDE, PAD), 1)
    for a in range(GROUP):
        row, offset = divmod(NG * a, PAD)
        value = rows[row]
        if offset + NG > PAD:
            value = jnp.where(lane >= offset, value, rows[row + 1])
        if offset:
            value = pltpu.roll(value, PAD - offset, 1)
        target[pl.ds(base + a, WIDE, stride=GROUP), :] = value


def gather(source, base, target):
    lane = lax.broadcasted_iota(jnp.int32, (WIDE, PAD), 1)
    rows = []
    for a in range(GROUP):
        value = source[pl.ds(base + a, WIDE, stride=GROUP), :]
        shift = NG * a % PAD
        rows.append(pltpu.roll(value, shift, 1) if shift else value)
    for j in range(5):
        low, high = PAD * j // NG, (PAD * j + PAD - 1) // NG
        value = rows[low]
        for a in range(low + 1, high + 1):
            value = jnp.where(lane >= NG * a - PAD * j, rows[a], value)
        target[pl.ds(j, WIDE, stride=5), :] = value


def flag(condition):
    return jnp.where(condition, 1, 0)


def encode(values, inverse):
    level = jnp.sqrt(jnp.abs(values) * inverse) * LEVELS
    whole = jnp.floor(level)
    code = jnp.exp2(whole - LEVELS / 2) * (1.0 + (level - whole))
    return jnp.where(values < 0.0, -code, code)


def decode(codes, scale):
    size = jnp.maximum(jnp.abs(codes), 2.0 ** (-LEVELS / 2))
    whole = jnp.floor(jnp.log2(size))
    level = (whole + (LEVELS / 2 - 1.0) + size * jnp.exp2(-whole)) * (1.0 / LEVELS)
    level = level * level * scale
    return jnp.where(codes < 0.0, -level, level)


def vectors_kernel(count, orbitals, forward_left, inverse_left, forward_right,
                   inverse_right, row_squares, lane_squares, vectors, total,
                   one, two, bands, targets_in, part, landed, wide, target, partners, padded, flat, outgoing, incoming,
                   own_partners, decoded, points, products, sums,
                   part_send, part_receive, target_send, target_receive, vector_send,
                   vector_receive, sum_send, sum_receive, own_sem, out_sem, load_sem):
    me = lax.axis_index("band")
    stride = count // NP
    layers = count // QUARTERS
    column = lax.rem(me, QUARTERS)
    layer = lax.div(me, QUARTERS)
    beside, behind = flip(me, 1), flip(me, 2)

    points_in = orbitals.shape[1]
    span = points_in // LOADS

    def loading(k):
        columns = pl.ds(k * span, span)
        return pltpu.make_async_copy(orbitals.at[:, columns], bands.at[:, columns], load_sem.at[k])

    for k in range(LOADS):
        loading(k).start()
    barrier = pltpu.get_barrier_semaphore()
    for step in range(1, count):
        pl.semaphore_signal(
            barrier, inc=1, device_id={"band": lax.rem(me + step, count)},
            device_id_type=pl.DeviceIdType.MESH,
        )
    at_root = [me == r * stride for r in range(NP)]

    def cut(n, row):
        size = CHUNK * PAD
        piece = bands[:, pl.ds(pl.multiple_of(n * size, PAD), size)].astype(jnp.float32)
        value = piece[row : row + 1].reshape(CHUNK, PAD)
        rest = jnp.zeros((HALF - CHUNK, PAD), jnp.float32)
        return jnp.concatenate([value, rest], axis=0)

    def take_row(n, carry):
        value = cut(n, orbitals.shape[0] - 1).astype(part.dtype)
        for r in range(NP):
            @pl.when(at_root[r])
            def _():
                part[r, n] = value
        return carry

    def take_target(n, carry):
        value = cut(n, 0)
        targets_in[n] = value.astype(targets_in.dtype)
        wide[0:HALF] = value
        spread(wide, target, pl.multiple_of(n * 200, 8))
        return carry

    for k in range(LOADS):
        loading(k).wait()
        pieces = (PIECES // LOADS * k, PIECES // LOADS * (k + 1))

        @pl.when(at_root[0] | at_root[1])
        def _():
            lax.fori_loop(*pieces, take_row, 0)

    pl.semaphore_wait(barrier, count - 1)

    def slab_of_target(mask):
        other = flip(me, mask)
        return remote(targets_in.at[pl.ds(2 * other, 2)], landed.at[pl.ds(2 * me, 2)],
                      target_send.at[mask], target_receive.at[mask], other)

    def own_target():
        return pltpu.make_async_copy(targets_in.at[pl.ds(2 * me, 2)], landed.at[pl.ds(2 * me, 2)],
                                     own_sem.at[1])

    def forward(r, n, way, other):
        unit = pl.ds(n * PER, PER)
        return remote(part.at[r, unit], part.at[r, unit], part_send.at[r, n, way],
                      part_receive.at[r, n], other)

    at_source = [layer == r * stride // QUARTERS for r in range(NP)]
    is_root = [me == r * stride for r in range(NP)]
    own_ways = [
        [
            jnp.where(at_source[r], lax.rem(me + d * QUARTERS, count), peer)
            for d, peer in ((1, beside), (2, behind), (3, flip(me, 3)))
        ]
        for r in range(NP)
    ]
    ends = (column == 0) | (column == QUARTERS - 1)
    hands = [ends | (column == (1, 1, 2, 3)[q]) for q in range(QUARTERS)]
    after = [jnp.where(ends if q < 2 else ~ends, beside, behind) for q in range(QUARTERS)]

    def start_all(r, c):
        for d, other in enumerate(own_ways[r]):
            forward(r, QUARTERS * c + column, d, other).start()

    def seed(r):
        def step(c, carry):
            for q in (3, 1, 2, 0):
                other = me + q if q == QUARTERS - 1 else after[q]
                forward(r, QUARTERS * c + q, 3, other).start()
            start_all(r, c)
            return carry

        lax.fori_loop(0, STEPS, step, 0)

    for r in range(NP):
        @pl.when(is_root[r])
        def _():
            seed(r)

    def wait_part(r, n):
        forward(r, n, 0, beside).wait_recv()

    def hand_on(r, i):
        c = i - late[r]

        @pl.when((c >= 0) & (c < STEPS) & ~is_root[r])
        def _():
            wait_part(r, QUARTERS * c + column)
            start_all(r, c)

            @pl.when(at_source[r])
            def _():
                for q in (3, 1, 2, 0):
                    @pl.when(hands[q])
                    def _():
                        @pl.when(column != q)
                        def _():
                            wait_part(r, QUARTERS * c + q)

                        forward(r, QUARTERS * c + q, 3, after[q]).start()
                        if q == QUARTERS - 1:
                            forward(r, QUARTERS * c + q, 4, beside).start()

    late = [flag(~at_source[r]) for r in range(NP)]
    still = [
        [~is_root[r] & (column != q) & ~(at_source[r] & hands[q]) for q in range(QUARTERS)]
        for r in range(NP)
    ]

    def receive_rest(r, c):
        for q in range(QUARTERS):
            @pl.when(still[r][q])
            def _():
                wait_part(r, QUARTERS * c + q)

    def ahead(step, carry):
        rows = pl.ds(pl.multiple_of(step * GROUP * NG, GROUP * NG), GROUP * NG)
        left = target[rows]
        parts = [right(left * partners[r, rows], forward_right[...]) for r in range(NP)]
        values = jnp.concatenate(parts, axis=1).reshape(GROUP, NG, NP * PAD)
        out = jnp.stack([from_left(forward_left[...], values[i]) for i in range(GROUP)])
        one[:, pl.ds(pl.multiple_of(step * GROUP, GROUP), GROUP), :] = jnp.swapaxes(out, 0, 1)
        return carry

    def relay(i, carry):
        for r in range(NP):
            hand_on(r, i)

        @pl.when(i < STEPS)
        def _():
            pieces = PIECES // STEPS
            lax.fori_loop(i * pieces, (i + 1) * pieces, take_target, 0)

        @pl.when(i == TARGETS_AT)
        def _():
            for mask in list(range(count // 2, count)) + list(range(1, count // 2)):
                slab_of_target(mask).start()
            own_target().start()

        @pl.when(i >= LAG)
        def _():
            c = i - LAG
            for r in range(NP):
                receive_rest(r, c)

            def arrived(q, carry):
                n = c * (QUARTERS * PER) + q
                for r in range(NP):
                    wide[0:HALF] = part[r, n].astype(jnp.float32)
                    spread(wide, partners.at[r], pl.multiple_of(n * 200, 8))
                return carry

            lax.fori_loop(0, QUARTERS * PER, arrived, 0)
            first, last = (lax.div(NG // STEPS * k, GROUP) for k in (c, c + 1))
            lax.fori_loop(first, last, ahead, 0)

        return carry

    lax.fori_loop(0, STEPS + LAG, relay, 0)

    def middle(step, carry):
        outs = []
        for i in range(GROUP):
            number = step * GROUP + i
            folded = jnp.where(number <= NG // 2, number, number - NG // 2)
            wave = (2.0 * np.pi / NG) * folded.astype(jnp.float32)
            totals = row_squares[...] + lane_squares[...] + wave * wave
            weight = jnp.where(totals > 0.0, 1.0 / (0.0025 + totals), 0.0)
            spectrum = from_left(forward_left[...], one[number]) * weight
            outs.append(from_left(inverse_left[...], spectrum))
        out = jnp.stack(outs)
        two[:, pl.ds(pl.multiple_of(step * GROUP, GROUP), GROUP), :] = jnp.swapaxes(out, 0, 1)
        return carry

    lax.fori_loop(0, NG // GROUP, middle, 0)

    planes = NG // count
    padded[pl.ds(planes * NG, 64)] = jnp.zeros((64, PAD), jnp.float32)

    def slab(mask):
        other = flip(me, mask)
        return remote(outgoing.at[other], incoming.at[me], vector_send.at[mask],
                      vector_receive.at[mask], other)

    def own_slab():
        return pltpu.make_async_copy(outgoing.at[me], incoming.at[me],
                                     own_sem.at[0])

    def back(step, carry):
        mask = lax.rem(step + count // 2, count)
        s = flip(me, mask)
        spectra = [two[s * planes + i] for i in range(planes)]
        side = jnp.zeros((1, PAD), jnp.float32)
        lane = lax.broadcasted_iota(jnp.int32, (1, PAD), 1)
        for i in range(planes):
            for r in range(NP):
                mean = spectra[i][0:1, r * PAD : r * PAD + 1] / NG
                side = jnp.where(lane == 8 * r + i, mean, side)
        row = lax.broadcasted_iota(jnp.int32, (NG, NP * PAD), 0)
        column = lax.broadcasted_iota(jnp.int32, (NG, NP * PAD), 1)
        keep = (row != 0) | ((column != 0) & (column != PAD))
        values = jnp.concatenate(
            [from_left(inverse_left[...], jnp.where(keep, x, 0.0)) for x in spectra], axis=0
        )
        rows = pl.ds(pl.multiple_of(s * planes * NG, planes * NG), planes * NG)
        result = jnp.zeros((planes * NG, PAD), jnp.float32)
        for r in range(NP):
            potential = right(values[:, r * PAD : (r + 1) * PAD], inverse_right[...])
            result -= partners[r, rows] * potential
        padded[0 : planes * NG] = result
        for h in range(2):
            gather(padded, h * 200, flat.at[pl.ds(h * HALF, 160)])
        biggest = jnp.max(jnp.abs(result), axis=0, keepdims=True)
        biggest = jnp.max(biggest, axis=1, keepdims=True)
        side = jnp.where(lane == 16, biggest, side)
        inverse = jnp.where(biggest > 0.0, 1.0 / biggest, 0.0)
        codes = encode(flat[0:SPAN], inverse)
        high = side.astype(jnp.bfloat16).astype(jnp.float32)
        rest = side - high
        middling = rest.astype(jnp.bfloat16).astype(jnp.float32)
        line = lax.broadcasted_iota(jnp.int32, (8, PAD), 0)
        last = codes[HALF - 8 : HALF]
        for i, value in ((CHUNK, high), (CHUNK + 1, middling), (CHUNK + 2, rest - middling)):
            last = jnp.where(line == i - HALF + 8, value, last)
        codes = jnp.concatenate([codes[: HALF - 8], last, codes[HALF:]], axis=0)
        outgoing[s] = codes.astype(outgoing.dtype)

        @pl.when(mask != 0)
        def _():
            slab(mask).start()

        @pl.when(mask == 0)
        def _():
            own_slab().start()

        return carry

    lax.fori_loop(0, count, back, 0)

    own_target().wait()
    for mask in range(1, count):
        slab_of_target(mask).wait()

    def lift(n, carry):
        points[pl.ds(pl.multiple_of(n * HALF, HALF), HALF)] = landed[n].astype(jnp.float32)
        return carry

    lax.fori_loop(0, PIECES, lift, 0)

    def sent(c, carry):
        for r in range(NP):
            for d, other in enumerate(own_ways[r]):
                forward(r, QUARTERS * c + column, d, other).wait_send()

            @pl.when(at_source[r])
            def _():
                for q in range(QUARTERS):
                    @pl.when(hands[q])
                    def _():
                        forward(r, QUARTERS * c + q, 3, after[q]).wait_send()
                        if q == QUARTERS - 1:
                            @pl.when(column == q)
                            def _():
                                forward(r, QUARTERS * c + q, 4, beside).wait_send()

        return carry

    lax.fori_loop(0, STEPS, sent, 0)

    for r in range(NP):
        for h in range(2):
            own_partners[r, h * HALF : (h + 1) * HALF] = part[r, 2 * me + h].astype(jnp.float32)
    line = lax.broadcasted_iota(jnp.int32, (SPAN, PAD), 0)
    plane = lax.div(line - flag(line >= HALF) * (HALF - CHUNK), NG * NG // PAD)

    def stored(b):
        return pltpu.make_async_copy(decoded.at[b], vectors.at[b], out_sem.at[b])

    def meet(mask, carry):
        @pl.when(mask != 0)
        def _():
            slab(mask).wait_recv()

        @pl.when(mask == 0)
        def _():
            own_slab().wait()

        b = flip(me, mask)
        codes = incoming[b].astype(jnp.float32)
        side = jnp.sum(codes[CHUNK:HALF], axis=0, keepdims=True)
        values = decode(codes, side[:, 16:17])
        for r in range(NP):
            mean = side[:, 8 * r : 8 * r + 1]
            for i in range(1, planes):
                mean = jnp.where(plane >= i, side[:, 8 * r + i : 8 * r + i + 1], mean)
            values -= own_partners[r] * mean
        decoded[b] = values
        stored(b).start()
        for a in range(count):
            product = points[a * SPAN : (a + 1) * SPAN] * values
            product = jnp.sum(product.reshape(SPAN // 8, 8, PAD), axis=0)
            products[pl.ds(b * count + a, 1)] = jnp.sum(product, axis=0, keepdims=True)
        return carry

    lax.fori_loop(0, count, meet, 0)

    line = jnp.sum(products[...], axis=1, keepdims=True)
    row = lax.broadcasted_iota(jnp.int32, (count * count, PAD), 0)
    lane = lax.broadcasted_iota(jnp.int32, (count * count, PAD), 1)
    placed = jnp.where(lane == lax.rem(row, count), line, 0.0)
    sums[me] = jnp.sum(placed.reshape(count, count, PAD), axis=1)

    def share_sum(mask):
        return remote(sums.at[me], sums.at[me], sum_send.at[mask], sum_receive.at[mask],
                      flip(me, mask))

    for mask in range(count - 1, 0, -1):
        share_sum(mask).start()
    for mask in range(1, count):
        slab(mask).wait_send()
    for mask in range(1, count):
        share_sum(mask).wait()
    total[...] = jnp.sum(sums[...], axis=0)
    for b in range(count):
        stored(b).wait()


def vectors_of(orbitals, count):
    fourier, squares = tables(NG)
    lanes = np.zeros((PAD,), np.float32)
    lanes[:NG] = squares
    vmem = pl.BlockSpec(memory_space=pltpu.VMEM)
    dma = pltpu.SemaphoreType.DMA
    cube = NG * NG + 64
    planes = NG // count
    return pl.pallas_call(
        functools.partial(vectors_kernel, count),
        out_shape=(
            jax.ShapeDtypeStruct((count, SPAN, PAD), jnp.float32),
            jax.ShapeDtypeStruct((count, PAD), jnp.float32),
        ),
        in_specs=[pl.BlockSpec(memory_space=pl.ANY)] + [vmem] * 6,
        out_specs=(pl.BlockSpec(memory_space=pl.ANY), vmem),
        scratch_shapes=[
            pltpu.VMEM((NG, NG, NP * PAD), jnp.float32),
            pltpu.VMEM((NG, NG, NP * PAD), jnp.float32),
            pltpu.VMEM(orbitals.shape, orbitals.dtype),
            pltpu.VMEM((PIECES, HALF, PAD), orbitals.dtype),
            pltpu.VMEM((NP, PIECES, HALF, PAD), orbitals.dtype),
            pltpu.VMEM((PIECES, HALF, PAD), orbitals.dtype),
            pltpu.VMEM((160, PAD), jnp.float32),
            pltpu.VMEM((cube, PAD), jnp.float32),
            pltpu.VMEM((NP, cube, PAD), jnp.float32),
            pltpu.VMEM((planes * NG + 64, PAD), jnp.float32),
            pltpu.VMEM((SPAN + 32, PAD), jnp.float32),
            pltpu.VMEM((count, SPAN, PAD), orbitals.dtype),
            pltpu.VMEM((count, SPAN, PAD), orbitals.dtype),
            pltpu.VMEM((NP, SPAN, PAD), jnp.float32),
            pltpu.VMEM((count, SPAN, PAD), jnp.float32),
            pltpu.VMEM((count * SPAN, PAD), jnp.float32),
            pltpu.VMEM((count * count, PAD), jnp.float32),
            pltpu.VMEM((count, count, PAD), jnp.float32),
            dma((NP, UNITS, 5)), dma((NP, UNITS)), dma((count,)), dma((count,)),
            dma((count,)), dma((count,)), dma((count,)), dma((count,)), dma((2,)), dma((count,)), dma((LOADS,)),
        ],
        compiler_params=pltpu.CompilerParams(
            collective_id=3, has_side_effects=True, vmem_limit_bytes=58 << 20
        ),
        cost_estimate=pl.CostEstimate(
            flops=12 * NP * NG**4, bytes_accessed=8 << 20, transcendentals=0
        ),
        name="vectors",
    )(
        orbitals,
        left_table(fourier),
        left_table(fourier.T.copy()),
        right_square(fourier.T.copy()),
        right_square(fourier),
        np.broadcast_to(squares[:, None], (NG, NP * PAD)).copy(),
        np.tile(lanes, NP)[None, :],
    )


def finish_kernel(total, vectors, projector, factors, mixed, held, made, load_sem, store_sem):
    count = total.shape[0]

    def load(h):
        rows = pl.ds(h * HALF, HALF)
        return pltpu.make_async_copy(vectors.at[:, rows], held.at[:, rows], load_sem.at[h])

    for h in range(2):
        load(h).start()
    scale = -0.5 / NG**3
    square = jnp.concatenate([total[...], jnp.zeros((PAD - count, PAD), jnp.float32)], axis=0)
    metric = scale * (square + square.T)[:count]
    row = lax.broadcasted_iota(jnp.int32, (count, PAD), 0)
    lane = lax.broadcasted_iota(jnp.int32, (count, PAD), 1)
    state = metric + jnp.where(lane == row + count, 1.0, 0.0)
    for k in range(count - 1):
        pivot = state[k : k + 1]
        ratio = state[:, k : k + 1] / pivot[:, k : k + 1]
        state = state - jnp.where(row > k, ratio, 0.0) * pivot
    diagonal = jnp.sum(jnp.where(lane == row, state, 0.0), axis=1, keepdims=True)
    state = state * (1.0 / jnp.sqrt(diagonal))
    for j in range(count):
        factors[j] = jnp.broadcast_to(state[:, count + j : count + j + 1], (count, PAD))

    size = 32
    blocks = HALF // size

    def store(h, step, lines):
        start = pl.multiple_of((h * CHUNK + step * size) * PAD, PAD)
        columns = pl.ds(start, lines * PAD)
        return pltpu.make_async_copy(made.at[:, columns], projector.at[:, columns],
                                     store_sem.at[h, step])

    for h in range(2):
        load(h).wait()

        def mix(step, carry):
            rows = pl.ds(pl.multiple_of(h * HALF + step * size, size), size)
            values = [held[j, rows] for j in range(count)]
            for k in range(count):
                result = factors[0, k : k + 1] * values[0]
                for j in range(1, k + 1):
                    result += factors[j, k : k + 1] * values[j]
                mixed[pl.ds(k, size, stride=count), :] = result
            for i in range(size):
                start = pl.multiple_of((h * CHUNK + step * size + i) * PAD, PAD)
                made[:, pl.ds(start, PAD)] = mixed[i * count : (i + 1) * count]

            @pl.when(step < blocks - 1)
            def _():
                store(h, step, size).start()

            return carry

        lax.fori_loop(0, blocks, mix, 0)
        store(h, blocks - 1, CHUNK - (blocks - 1) * size).start()
    for h in range(2):
        for step in range(blocks - 1):
            store(h, step, size).wait()
        store(h, blocks - 1, CHUNK - (blocks - 1) * size).wait()


def finish(total, vectors):
    count = total.shape[0]
    vmem = pl.BlockSpec(memory_space=pltpu.VMEM)
    anywhere = pl.BlockSpec(memory_space=pl.ANY)
    return pl.pallas_call(
        finish_kernel,
        out_shape=jax.ShapeDtypeStruct((count, 2 * CHUNK * PAD), jnp.float32),
        in_specs=[vmem, anywhere],
        out_specs=anywhere,
        scratch_shapes=[
            pltpu.VMEM((count, count, PAD), jnp.float32),
            pltpu.VMEM((32 * count, PAD), jnp.float32),
            pltpu.VMEM(vectors.shape, jnp.float32),
            pltpu.VMEM((count, (SPAN + 8) * PAD), jnp.float32),
            pltpu.SemaphoreType.DMA((2,)),
            pltpu.SemaphoreType.DMA((2, 4)),
        ],
        compiler_params=pltpu.CompilerParams(vmem_limit_bytes=60 << 20),
        name="finish",
    )(total, vectors)


def fast_body(orbitals):
    vectors, total = vectors_of(orbitals, lax.axis_size("band"))
    return finish(total, vectors)


def body(orbitals):
    devices = lax.axis_size("band")
    points = orbitals.shape[1]
    target, row = pick(orbitals)
    partners = share(row.reshape(QUARTERS, CHUNKS, -1, PAD), devices)
    vectors, target_slab = exchange(
        target.reshape(NG, NG, NG),
        partners.reshape(NP, NG, NG, NG),
        target.reshape(devices, 8, points // devices // 8),
        devices,
    )
    vector_slab = lax.all_to_all(
        vectors.reshape(1, points), "band", split_axis=1, concat_axis=0, tiled=True
    )
    target_slab = target_slab.reshape(devices, points // devices).astype(jnp.float32)
    part = jnp.einsum("ap,bp->ab", target_slab, vector_slab, precision=highest) / NG**3
    intersection = sum_all(part, devices)
    metric = -0.5 * (intersection + intersection.T)
    factor = lax.linalg.cholesky(metric, symmetrize_input=False)
    return jax.scipy.linalg.solve_triangular(factor, vector_slab, lower=True)


def solution(mesh):
    placed = (P(("spin", "band"), None),)
    fast = mesh.shape["band"] == 2 * NP * QUARTERS
    return jax.shard_map(
        fast_body if fast else body, mesh=mesh, in_specs=placed, out_specs=P("spin", "band"), check_vma=False
    )
```
